32 devices in a mesh: band: 4 (over y, x), pair: 8 (over z, core).
Axes of the slice: x: 2, y: 2, z: 4, core: 2. Of those that a mesh axis runs over, the one named last changes fastest.
Arguments:
- visibilities: float32 [4, 16, 8, 2, 1024], P('band', 'pair'), may hold values from -6 to 6
- coherencies: bfloat16 [4, 16, 8, 2, 32, 1024], P('band', 'pair'), may hold values from -1 to 1
- block_tiles: int32 [16, 2], P('pair'), may hold values from 0 to 15, as said below
- sample_counts: int32 [16], P('pair'), may hold values from 1 to 8, as said below
- gains: float32 [4, 2, 32, 512], P('band', None, None, 'pair'), may hold values from 0.5 to 1.5
- targets: float32 [4, 2, 32, 512], P('band', None, None, 'pair'), may hold values from 0.5 to 1.5
- multipliers: float32 [4, 2, 32, 512], P('band', None, None, 'pair'), may hold values from -2 to 2
Outputs:
- new_gains: float32 [4, 2, 32, 512], P('band', None, None, 'pair')
- new_targets: float32 [4, 2, 32, 512], P('band', None, None, 'pair')
- new_multipliers: float32 [4, 2, 32, 512], P('band', None, None, 'pair')
The draws below stay inside these ranges and needn't reach their ends.
Inputs may be any that keep to these rules, and one draw needn't show every extreme that they name: `block_tiles`: each row names two station tiles a <= b; no tile pair appears twice; the pairs (0, 15) and (15, 15) are always among them. `sample_counts`: some block has all 8 samples and some block only one.
All inputs are finite; a program needn't handle non-finite values.
Results may differ from the reference program's by a relative error of at most 0.0003.
Values sent between devices are 32-bit elements; how exact they have to be, the bound alone decides.
No kernel may reach another device: no remote copies, remote signals or barrier semaphores. Data moves between devices by JAX's collectives and lax.ppermute only.
A program may use at most 64 MiB of HBM per device.

```python
import math
import jax
import jax.numpy as jnp
from jax import lax

S = 512
K = 32
P_SIZE = 8
TILE = 32
ITERS = 2
TIMES = 8
NTILE = 16
BLK = 1024
NBLK = 16
F = 4


def draw_block_tiles(key, part):
    pair_index = jnp.arange(NTILE * NTILE)
    first = pair_index // NTILE
    second = pair_index % NTILE
    shuffled = jax.random.permutation(key, NTILE * NTILE)
    ranking = jnp.where(first <= second, 1, 2)
    ranking = jnp.where((first == 0) & (second == NTILE - 1), 0, ranking)
    ranking = jnp.where((first == NTILE - 1) & (second == NTILE - 1), 0, ranking)
    ordering = jnp.argsort(ranking[shuffled], stable=True)
    chosen = shuffled[ordering[:NBLK]]
    mixing = jax.random.permutation(jax.random.fold_in(key, 7), NBLK)
    chosen = chosen[mixing]
    return jnp.stack([chosen // NTILE, chosen % NTILE], axis=1).astype(jnp.int32)


def draw_sample_counts(key, part):
    counts = jax.random.randint(key, (NBLK,), 1, TIMES + 1)
    spot_full = jax.random.randint(jax.random.fold_in(key, 3), (), 0, NBLK)
    offset = jax.random.randint(jax.random.fold_in(key, 5), (), 1, NBLK)
    spot_single = (spot_full + offset) % NBLK
    counts = counts.at[spot_full].set(TIMES)
    counts = counts.at[spot_single].set(1)
    return counts.astype(jnp.int32)


def steps_of(key, extent, shards, least, high):
    factor_of, own = 1.0, jax.random.fold_in(key, 6)
    for position, parts in shards:
        draws = jnp.exp(jax.random.uniform(jax.random.fold_in(own, position), (parts,), jnp.float32, least / len(shards), high / len(shards)))
        factor_of = factor_of * jnp.repeat(draws, extent[position] // parts).reshape([-1 if axis == position else 1 for axis in range(len(extent))])
    return factor_of


def bell_draw(key, shape, deviation, most, split=(), held_as=jnp.bfloat16):
    values = deviation * jax.random.normal(key, shape, jnp.float32)
    if split:
        values = values * steps_of(key, shape, split, -0.22, 0.18)
    return jnp.clip(values, -most, most).astype(held_as)


def setup_inputs(seed: int = 0) -> dict:
    streams_of = jax.random.split(jax.random.key(seed), 8)
    return {
        "visibilities": bell_draw(streams_of[0], (F, NBLK, TIMES, 2, BLK), 1.0, 6.0, ((0, 4), (1, 8)), jnp.float32),
        "coherencies": bell_draw(streams_of[1], (F, NBLK, TIMES, 2, K, BLK), K ** -0.5, 1.0, ((0, 4), (1, 8))),
        "block_tiles": draw_block_tiles(jax.random.fold_in(streams_of[7], 71), 0),
        "sample_counts": draw_sample_counts(jax.random.fold_in(streams_of[7], 71), 0),
        "gains": jnp.clip(0.5 + 1.0 * jax.random.uniform(streams_of[4], (F, 2, K, S), jnp.float32) ** steps_of(streams_of[4], (F, 2, K, S), ((0, 4), (3, 8)), -0.2, 0.2), 0.5, 1.5),
        "targets": jnp.clip(0.5 + 1.0 * jax.random.uniform(streams_of[5], (F, 2, K, S), jnp.float32) ** steps_of(streams_of[5], (F, 2, K, S), ((0, 4), (3, 8)), -0.2, 0.2), 0.5, 1.5),
        "multipliers": bell_draw(streams_of[6], (F, 2, K, S), 0.3, 2.0, ((0, 4), (3, 8)), jnp.float32),
    }


ridge = 0.05
penalty = 0.25

def bernstein_table(freq_count, term_count):
    positions = (jnp.arange(freq_count).astype(jnp.float32) + 0.5) / freq_count
    columns = [math.comb(term_count - 1, degree) * positions ** degree * (1.0 - positions) ** (term_count - 1 - degree) for degree in range(term_count)]
    return jnp.stack(columns, axis=1)

def block_terms(gains_first, gains_second, vis_block, coh_block, same_tile, valid_count):
    tile_width = gains_first.shape[-1]
    left_gains = jnp.repeat(gains_first, tile_width, axis=-1)
    right_gains = jnp.tile(gains_second, (1, 1, tile_width))
    prod_real = left_gains[0] * right_gains[0] + left_gains[1] * right_gains[1]
    prod_imag = left_gains[1] * right_gains[0] - left_gains[0] * right_gains[1]
    cohere = coh_block.astype(jnp.float32)
    coh_real = cohere[:, 0]
    coh_imag = cohere[:, 1]
    model_real = jnp.sum(prod_real[None] * coh_real - prod_imag[None] * coh_imag, axis=1)
    model_imag = jnp.sum(prod_real[None] * coh_imag + prod_imag[None] * coh_real, axis=1)
    sample_total = vis_block.shape[0]
    cell_index = jnp.arange(tile_width * tile_width)
    row_index = cell_index // tile_width
    col_index = cell_index % tile_width
    keep_cell = (row_index < col_index) | jnp.logical_not(same_tile)
    keep_time = jnp.arange(sample_total) < valid_count
    weight = (keep_time[:, None] & keep_cell[None, :]).astype(jnp.float32)
    res_real = (vis_block[:, 0] - model_real) * weight
    res_imag = (vis_block[:, 1] - model_imag) * weight
    acc_real = jnp.sum(res_real[:, None] * coh_real + res_imag[:, None] * coh_imag, axis=0)
    acc_imag = jnp.sum(res_imag[:, None] * coh_real - res_real[:, None] * coh_imag, axis=0)
    term_real = acc_real * right_gains[0] - acc_imag * right_gains[1]
    term_imag = acc_real * right_gains[1] + acc_imag * right_gains[0]
    direction_count = acc_real.shape[0]
    grad_first = -jnp.stack([term_real, term_imag]).reshape(2, direction_count, tile_width, tile_width).sum(axis=3)
    other_real = acc_real * left_gains[0] + acc_imag * left_gains[1]
    other_imag = acc_real * left_gains[1] - acc_imag * left_gains[0]
    grad_second = -jnp.stack([other_real, other_imag]).reshape(2, direction_count, tile_width, tile_width).sum(axis=2)
    return (grad_first, grad_second)

def data_gradient(gain_band, vis_band, coh_band, block_tiles, sample_counts):
    direction_count = gain_band.shape[1]
    station_count = gain_band.shape[2]
    tile_count = station_count // TILE
    tile_range = jnp.arange(tile_count)
    onehot_first = (block_tiles[:, 0:1] == tile_range[None, :]).astype(jnp.float32)
    onehot_second = (block_tiles[:, 1:2] == tile_range[None, :]).astype(jnp.float32)
    grid = gain_band.reshape(2, direction_count, tile_count, TILE)
    tiles_first = jnp.einsum('bn,cknt->bckt', onehot_first, grid, precision=lax.Precision.HIGHEST)
    tiles_second = jnp.einsum('bn,cknt->bckt', onehot_second, grid, precision=lax.Precision.HIGHEST)
    same_tile = block_tiles[:, 0] == block_tiles[:, 1]

    def one_block(packed):
        return block_terms(*packed)
    grad_first, grad_second = lax.map(one_block, (tiles_first, tiles_second, vis_band, coh_band, same_tile, sample_counts))
    total = jnp.einsum('bn,bckt->cknt', onehot_first, grad_first, precision=lax.Precision.HIGHEST)
    total = total + jnp.einsum('bn,bckt->cknt', onehot_second, grad_second, precision=lax.Precision.HIGHEST)
    return total.reshape(2, direction_count, station_count)

def reference(visibilities, coherencies, block_tiles, sample_counts, gains, targets, multipliers):
    step_size = 0.25 * NTILE * K / (TIMES * TILE * NBLK)

    def one_band(packed):
        vis_band, coh_band, gain_band, target_band, mult_band = packed
        for iteration in range(ITERS):
            gradient = data_gradient(gain_band, vis_band, coh_band, block_tiles, sample_counts)
            gain_band = gain_band - step_size * gradient - penalty * (gain_band - target_band + mult_band)
        return gain_band
    new_gains = lax.map(one_band, (visibilities, coherencies, gains, targets, multipliers))
    basis_table = bernstein_table(F, P_SIZE)
    normal = jnp.dot(basis_table.T, basis_table, precision=lax.Precision.HIGHEST) + ridge * jnp.eye(P_SIZE, dtype=jnp.float32)
    factor = jnp.linalg.cholesky(normal)
    summed = (new_gains + multipliers).reshape(F, -1)
    moments = jnp.dot(basis_table.T, summed, precision=lax.Precision.HIGHEST)
    coeffs = jax.scipy.linalg.cho_solve((factor, True), moments)
    new_targets = jnp.dot(basis_table, coeffs, precision=lax.Precision.HIGHEST).reshape(new_gains.shape)
    new_multipliers = multipliers + new_gains - new_targets
    return (new_gains, new_targets, new_multipliers)
```

```python
import math

import jax
import jax.numpy as jnp
import numpy as np
from jax import lax
from jax.experimental import pallas as pl
from jax.experimental.pallas import tpu as pltpu
from jax.sharding import PartitionSpec as P

P_SIZE = 8
TILE = 32
LANES = 128
CHUNKS = 2

ridge = 0.05
penalty = 0.25


def fit_matrix(freq_count, term_count):
    positions = (np.arange(freq_count) + 0.5) / freq_count
    basis = np.stack(
        [
            math.comb(term_count - 1, degree)
            * positions**degree
            * (1.0 - positions) ** (term_count - 1 - degree)
            for degree in range(term_count)
        ],
        axis=1,
    )
    normal = basis.T @ basis + ridge * np.eye(term_count)
    factor = np.linalg.cholesky(normal)
    half = np.linalg.solve(factor, basis.T)
    return half.T @ half


class Plan:
    def __init__(self, directions, stations, pairs, blocks):
        self.k = directions
        self.sl = stations
        self.pairs = pairs
        self.zn = pairs // 2
        self.blocks = blocks
        self.width = max(LANES, 2 * stations)
        self.per = stations // TILE
        self.parts = 1 if self.per else TILE // stations
        self.rows = 2 * directions + 8 * ((blocks + 7) // 8)

    def owner(self, me, device):
        return (device % 2) == (me % 2), (device // 2) ^ (me // 2)

    def pad(self, pieces):
        have = sum(p.shape[1] for p in pieces)
        if have < self.width:
            pieces = pieces + [jnp.zeros((self.k, self.width - have), jnp.float32)]
        return jnp.concatenate(pieces, axis=1)

    def record(self, me, own_ref, sib_ref, device, row):
        same, slot = self.owner(me, device)
        own = own_ref[slot, row : row + self.k, :]
        sib = sib_ref[slot, row : row + self.k, :]
        return jnp.where(same, own, sib)

    def fetch(self, me, own_ref, sib_ref, tile, row):
        sl = self.sl
        if self.per:
            device = tile // self.per
            sub = tile - device * self.per
            rec = self.record(me, own_ref, sib_ref, device, row)
            real, imag = rec[:, :TILE], rec[:, sl : sl + TILE]
            for s in range(1, self.per):
                real = jnp.where(sub == s, rec[:, s * TILE : (s + 1) * TILE], real)
                imag = jnp.where(sub == s, rec[:, sl + s * TILE : sl + (s + 1) * TILE], imag)
            return real, imag
        recs = [
            self.record(me, own_ref, sib_ref, tile * self.parts + r, row)
            for r in range(self.parts)
        ]
        real = jnp.concatenate([rec[:, :sl] for rec in recs], axis=1)
        imag = jnp.concatenate([rec[:, sl : 2 * sl] for rec in recs], axis=1)
        return real, imag

    def spread(self, me, tile, real, imag, own_ref, sib_ref):
        if self.per:
            device = tile // self.per
            sub = tile - device * self.per
            none = jnp.zeros_like(real)
            placed = None
            for s in range(self.per):
                lay = [none] * self.per
                lay_imag = [none] * self.per
                lay[s], lay_imag[s] = real, imag
                here = self.pad(lay + lay_imag)
                placed = here if placed is None else jnp.where(sub == s, here, placed)
            targets = [(device, placed)]
        else:
            sl = self.sl
            targets = [
                (
                    tile * self.parts + r,
                    self.pad([real[:, r * sl : (r + 1) * sl], imag[:, r * sl : (r + 1) * sl]]),
                )
                for r in range(self.parts)
            ]
        for device, value in targets:
            same, slot = self.owner(me, device)
            own_ref[slot] = own_ref[slot] + jnp.where(same, value, 0.0)
            sib_ref[slot] = sib_ref[slot] + jnp.where(same, 0.0, value)


def pack_kernel(plan, tiles_ref, gains_ref, targets_ref, mult_ref, out_ref):
    k = plan.k
    gain = plan.pad([gains_ref[0, 0], gains_ref[0, 1]])
    target = plan.pad([targets_ref[0, 0], targets_ref[0, 1]])
    mult = plan.pad([mult_ref[0, 0], mult_ref[0, 1]])
    out_ref[:k] = gain
    out_ref[k : 2 * k] = gain - penalty * (gain - target + mult)
    lane = lax.broadcasted_iota(jnp.int32, (8, plan.width), 1)
    sub = lax.broadcasted_iota(jnp.int32, (8, plan.width), 0)
    for base in range(0, plan.blocks, 8):
        rows = jnp.zeros((8, plan.width), jnp.int32)
        for n in range(base, min(base + 8, plan.blocks)):
            ids = jnp.where(lane < 2 * TILE, tiles_ref[n, 0], tiles_ref[n, 1])
            rows = jnp.where(sub == n - base, ids, rows)
        out_ref[2 * k + base : 2 * k + base + 8] = rows.astype(jnp.float32)


def coherency_copies(plan, coh_ref, coh_buf, sems):
    cells = coh_buf.shape[-1] // CHUNKS
    copies = []
    for n in range(plan.blocks):
        for c in range(CHUNKS):
            lanes = pl.ds(c * cells, cells)
            copies.append(
                pltpu.make_async_copy(
                    coh_ref.at[0, n, :, :, :, lanes],
                    coh_buf.at[n, :, :, :, lanes],
                    sems.at[n * CHUNKS + c],
                )
            )
    return copies


def split_dot(lhs, rhs):
    total = None
    for _ in range(3):
        part = lhs.astype(jnp.bfloat16)
        value = jnp.dot(part, rhs, preferred_element_type=jnp.float32)
        total = value if total is None else total + value
        lhs = lhs - part.astype(jnp.float32)
    return total


def block_gradients(plan, tiles_ref, counts_ref, tile_gains, vis_ref, coh_buf, copies, fold_ref):
    k = plan.k
    times = coh_buf.shape[1]
    cells = coh_buf.shape[-1]
    groups = LANES // TILE
    steps = cells // LANES
    lane = lax.broadcasted_iota(jnp.int32, (1, LANES), 1)
    lane_k = lax.broadcasted_iota(jnp.int32, (k, LANES), 1)
    seconds = []
    for n in range(plan.blocks):
        (a_re, a_im), (b_re, b_im) = tile_gains[n]
        rr = jnp.concatenate([b_re] * groups, axis=1)
        ri = jnp.concatenate([b_im] * groups, axis=1)
        a_re4 = jnp.concatenate([a_re] * groups, axis=1)
        a_im4 = jnp.concatenate([a_im] * groups, axis=1)
        differ = tiles_ref[n, 0] != tiles_ref[n, 1]
        count = counts_ref[n]

        def step(index, carry, n=n, rr=rr, ri=ri, a_re4=a_re4, a_im4=a_im4):
            o_re, o_im = carry
            lanes = pl.ds(pl.multiple_of(index * LANES, LANES), LANES)
            pick = index * groups + lane_k // TILE
            lr = jnp.take_along_axis(a_re4, pick, axis=1, mode="promise_in_bounds")
            li = jnp.take_along_axis(a_im4, pick, axis=1, mode="promise_in_bounds")
            pr = lr * rr + li * ri
            pi = li * rr - lr * ri
            row = index * groups + lane // TILE
            keep = jnp.where(row < lane % TILE, 1, 0)
            keep = jnp.where(differ, 1, keep)
            acc_re = jnp.zeros((k, LANES), jnp.float32)
            acc_im = jnp.zeros((k, LANES), jnp.float32)
            for t in range(times):
                cr = coh_buf[n, t, 0, :, lanes].astype(jnp.float32)
                ci = coh_buf[n, t, 1, :, lanes].astype(jnp.float32)
                mr = jnp.sum(pr * cr - pi * ci, axis=0, keepdims=True)
                mi = jnp.sum(pr * ci + pi * cr, axis=0, keepdims=True)
                v = vis_ref[0, n, t, :, lanes]
                weight = jnp.where(t < count, keep, 0) > 0
                er = jnp.where(weight, v[0:1] - mr, 0.0)
                ei = jnp.where(weight, v[1:2] - mi, 0.0)
                acc_re = acc_re + (er * cr + ei * ci)
                acc_im = acc_im + (ei * cr - er * ci)
            fold_ref[2 * n * k : (2 * n + 1) * k, lanes] = acc_re * rr - acc_im * ri
            fold_ref[(2 * n + 1) * k : (2 * n + 2) * k, lanes] = acc_re * ri + acc_im * rr
            o_re = o_re + (acc_re * lr + acc_im * li)
            o_im = o_im + (acc_re * li - acc_im * lr)
            return o_re, o_im

        carry = (jnp.zeros((k, LANES), jnp.float32), jnp.zeros((k, LANES), jnp.float32))
        per_chunk = steps // CHUNKS
        for c in range(CHUNKS):
            copies[n * CHUNKS + c].wait()
            carry = lax.fori_loop(c * per_chunk, (c + 1) * per_chunk, step, carry)
        parts = []
        for o in carry:
            total = o[:, :TILE]
            for g in range(1, groups):
                total = total + o[:, g * TILE : (g + 1) * TILE]
            parts.append(total)
        seconds.append(parts)
    row = lax.broadcasted_iota(jnp.int32, (cells, TILE), 0)
    col = lax.broadcasted_iota(jnp.int32, (cells, TILE), 1)
    pool = jnp.where(row // TILE == col, 1.0, 0.0).astype(jnp.bfloat16)
    first = split_dot(fold_ref[...], pool)
    return [
        (
            first[2 * n * k : (2 * n + 1) * k],
            first[(2 * n + 1) * k : (2 * n + 2) * k],
            seconds[n][0],
            seconds[n][1],
        )
        for n in range(plan.blocks)
    ]


def first_kernel(plan, tiles_ref, counts_ref, own_ref, sib_ref, vis_ref, coh_ref, out_ref, coh_buf, fold_ref, sems):
    me = lax.axis_index("pair")
    copies = coherency_copies(plan, coh_ref, coh_buf, sems)
    for copy in copies:
        copy.start()
    tile_gains = [
        [plan.fetch(me, own_ref, sib_ref, tiles_ref[n, side], 0) for side in range(2)]
        for n in range(plan.blocks)
    ]
    grads = block_gradients(plan, tiles_ref, counts_ref, tile_gains, vis_ref, coh_buf, copies, fold_ref)
    for n, parts in enumerate(grads):
        out_ref[n] = jnp.concatenate(parts, axis=1)


def second_kernel(
    plan, step_size, tiles_ref, counts_ref, own_ref, sib_ref, term_own_ref, term_sib_ref, mult_ref, vis_ref, coh_ref,
    part_own_ref, part_sib_ref, rest_ref, coh_buf, fold_ref, sems,
):
    k, sl = plan.k, plan.sl
    me = lax.axis_index("pair")
    copies = coherency_copies(plan, coh_ref, coh_buf, sems)
    for copy in copies:
        copy.start()
    wanted = [tiles_ref[n, side] for n in range(plan.blocks) for side in range(2)]
    if plan.per:
        wanted += [me * plan.per + s for s in range(plan.per)]
    else:
        wanted += [me // plan.parts]
    labels = [t.astype(jnp.float32) for t in wanted]

    def gather(slot, sums):
        for pay_ref, term_ref in ((own_ref, term_own_ref), (sib_ref, term_sib_ref)):
            ids_all = pay_ref[slot, 2 * k : plan.rows, :]
            for n in range(plan.blocks):
                ids = ids_all[n : n + 1, : 4 * TILE]
                terms = term_ref[slot, n]
                sums = [s + jnp.where(ids == label, terms, 0.0) for s, label in zip(sums, labels)]
        return sums

    sums = [jnp.zeros((k, 4 * TILE), jnp.float32) for _ in wanted]
    if plan.zn <= 4:
        for slot in range(plan.zn):
            sums = gather(slot, sums)
    else:
        sums = lax.fori_loop(0, plan.zn, gather, sums)
    sums = [s[:, : 2 * TILE] + s[:, 2 * TILE :] for s in sums]

    tile_gains = []
    for n in range(plan.blocks):
        sides = []
        for side in range(2):
            real, imag = plan.fetch(me, own_ref, sib_ref, tiles_ref[n, side], k)
            total = sums[2 * n + side]
            sides.append((real + step_size * total[:, :TILE], imag + step_size * total[:, TILE:]))
        tile_gains.append(sides)

    mine = sums[2 * plan.blocks :]
    if plan.per:
        own_sum = plan.pad([s[:, :TILE] for s in mine] + [s[:, TILE:] for s in mine])
    else:
        spot = me % plan.parts
        real, imag = mine[0][:, :sl], mine[0][:, TILE : TILE + sl]
        for r in range(1, plan.parts):
            real = jnp.where(spot == r, mine[0][:, r * sl : (r + 1) * sl], real)
            imag = jnp.where(spot == r, mine[0][:, TILE + r * sl : TILE + (r + 1) * sl], imag)
        own_sum = plan.pad([real, imag])
    start = own_ref[0, :k, :]
    base = own_ref[0, k : 2 * k, :]
    pull = base - (1.0 - penalty) * start
    rest = (1.0 - penalty) * (base + step_size * own_sum) + pull
    rest_ref[0] = rest
    rest_ref[1] = rest + plan.pad([mult_ref[0, 0], mult_ref[0, 1]])

    grads = block_gradients(plan, tiles_ref, counts_ref, tile_gains, vis_ref, coh_buf, copies, fold_ref)
    part_own_ref[...] = jnp.zeros_like(part_own_ref)
    part_sib_ref[...] = jnp.zeros_like(part_sib_ref)
    for n, (f_re, f_im, s_re, s_im) in enumerate(grads):
        plan.spread(me, tiles_ref[n, 0], f_re, f_im, part_own_ref, part_sib_ref)
        plan.spread(me, tiles_ref[n, 1], s_re, s_im, part_own_ref, part_sib_ref)


def fit_kernel(plan, fit, gain_ref, own_ref, *refs):
    others, (gain_out, target_out, mult_out) = refs[:-3], refs[-3:]
    sl = plan.sl
    band = lax.axis_index("band")
    total = None
    for m, ref in enumerate((own_ref,) + tuple(others)):
        factor = jnp.float32(0.0)
        for f in range(fit.shape[0]):
            factor = jnp.where(band == f, jnp.float32(fit[f, f ^ m]), factor)
        value = factor * ref[...]
        total = value if total is None else total + value
    change = own_ref[...] - total
    gain = gain_ref[...]
    for part in range(2):
        lanes = slice(part * sl, (part + 1) * sl)
        gain_out[0, part] = gain[:, lanes]
        target_out[0, part] = total[:, lanes]
        mult_out[0, part] = change[:, lanes]


def exchange(value, axis, size, mask):
    return lax.ppermute(value, axis, [(i, i ^ mask) for i in range(size)])


def local(visibilities, coherencies, block_tiles, sample_counts, gains, targets, multipliers):
    pairs = lax.axis_size("pair")
    bands = lax.axis_size("band")
    _, blocks, times, _, directions, cells = coherencies.shape
    stations = gains.shape[3]
    plan = Plan(directions, stations, pairs, blocks)
    k, zn, width = plan.k, plan.zn, plan.width
    tile_count = stations * pairs // TILE
    step_size = 0.25 * tile_count * k / (times * TILE * blocks * pairs)

    smem = pl.BlockSpec(memory_space=pltpu.SMEM)
    vmem = pl.BlockSpec(memory_space=pltpu.VMEM)
    anywhere = pl.BlockSpec(memory_space=pl.ANY)
    f32 = lambda *shape: jax.ShapeDtypeStruct(shape, jnp.float32)
    scratch = [
        pltpu.VMEM((blocks, times, 2, k, cells), jnp.bfloat16),
        pltpu.VMEM((2 * blocks * k, cells), jnp.float32),
        pltpu.SemaphoreType.DMA((blocks * CHUNKS,)),
    ]
    params = pltpu.CompilerParams(vmem_limit_bytes=16 << 20)

    payload = pl.pallas_call(
        lambda *refs: pack_kernel(plan, *refs),
        name="pack",
        in_specs=[smem, vmem, vmem, vmem],
        out_specs=vmem,
        out_shape=f32(plan.rows, width),
        compiler_params=params,
    )(block_tiles, gains, targets, multipliers)

    def gather(value):
        parts = [value] + [exchange(value, "pair", pairs, 2 * m) for m in range(1, zn)]
        own = jnp.stack(parts)
        return own, exchange(own, "pair", pairs, 1)

    own, sib = gather(payload)
    terms = pl.pallas_call(
        lambda *refs: first_kernel(plan, *refs),
        name="first",
        in_specs=[smem, smem, vmem, vmem, vmem, anywhere],
        out_specs=vmem,
        out_shape=f32(blocks, k, 4 * TILE),
        scratch_shapes=scratch,
        compiler_params=params,
    )(block_tiles, sample_counts, own, sib, visibilities, coherencies)

    term_own, term_sib = gather(terms)
    part_own, part_sib, rest = pl.pallas_call(
        lambda *refs: second_kernel(plan, step_size, *refs),
        name="second",
        in_specs=[smem, smem, vmem, vmem, vmem, vmem, vmem, vmem, anywhere],
        out_specs=[vmem, vmem, vmem],
        out_shape=[f32(zn, k, width), f32(zn, k, width), f32(2, k, width)],
        scratch_shapes=scratch,
        compiler_params=params,
    )(block_tiles, sample_counts, own, sib, term_own, term_sib, multipliers, visibilities, coherencies)

    crossed = exchange(part_sib, "pair", pairs, 1)
    total = part_own[0] + crossed[0]
    for m in range(1, zn):
        total = total + exchange(part_own[m] + crossed[m], "pair", pairs, 2 * m)
    new_gain = rest[0] + step_size * total
    summed = rest[1] + step_size * total

    others = [exchange(summed, "band", bands, m) for m in range(1, bands)]
    shape = f32(*gains.shape)
    return pl.pallas_call(
        lambda *refs: fit_kernel(plan, fit_matrix(bands, P_SIZE), *refs),
        name="fit",
        in_specs=[vmem] * (2 + len(others)),
        out_specs=[vmem] * 3,
        out_shape=[shape] * 3,
        compiler_params=params,
    )(new_gain, summed, *others)


def solution(mesh):
    placed = (
        P("band", "pair", None, None, None),
        P("band", "pair", None, None, None, None),
        P("pair", None),
        P("pair"),
        P("band", None, None, "pair"),
        P("band", None, None, "pair"),
        P("band", None, None, "pair"),
    )
    return jax.shard_map(
        local,
        mesh=mesh,
        in_specs=placed,
        out_specs=(
            P("band", None, None, "pair"),
            P("band", None, None, "pair"),
            P("band", None, None, "pair"),
        ),
        check_vma=False,
    )
```

```python
import math

import jax
import jax.numpy as jnp
import numpy as np
from jax import lax
from jax.experimental import pallas as pl
from jax.experimental.pallas import tpu as pltpu
from jax.sharding import PartitionSpec as P


P_SIZE = 8
TILE = 32
LANES = 128
GROUP = LANES // TILE

ridge = 0.05
penalty = 0.25


def fit_matrix(freq_count, term_count):
    positions = (np.arange(freq_count) + 0.5) / freq_count
    basis = np.stack(
        [
            math.comb(term_count - 1, degree)
            * positions**degree
            * (1.0 - positions) ** (term_count - 1 - degree)
            for degree in range(term_count)
        ],
        axis=1,
    )
    normal = basis.T @ basis + ridge * np.eye(term_count)
    factor = np.linalg.cholesky(normal)
    half = np.linalg.solve(factor, basis.T)
    return half.T @ half


class Plan:
    def __init__(self, directions, stations, pairs, blocks, times, cells):
        self.k = directions
        self.sl = stations
        self.zn = pairs // 2
        self.blocks = blocks
        self.times = times
        self.cells = cells
        self.steps = cells // LANES
        self.per = stations // TILE
        self.parts = 1 if self.per else TILE // stations
        self.rows = 2 * directions + 8 * ((blocks + 7) // 8)
        assert 2 * stations <= LANES and directions == 32 and times <= 8 and self.steps == 8

    def lane(self, rows=None):
        return lax.broadcasted_iota(jnp.int32, (self.k if rows is None else rows, LANES), 1)

    def owner(self, me, device):
        return (device % 2) == (me % 2), (device // 2) ^ (me // 2)

    def record(self, me, own_ref, sib_ref, device, row):
        same, slot = self.owner(me, device)
        own = own_ref[slot, row : row + self.k, :]
        sib = sib_ref[slot, row : row + self.k, :]
        return jnp.where(same, own, sib)

    def fetch(self, me, own_ref, sib_ref, tile, row):
        lane = self.lane()
        part, spot = lane // TILE % 2, lane % TILE
        if self.per:
            device = tile // self.per
            sub = tile - device * self.per
            rec = self.record(me, own_ref, sib_ref, device, row)
            return take(rec, part * self.sl + sub * TILE + spot)
        value = None
        for r in range(self.parts):
            rec = self.record(me, own_ref, sib_ref, tile * self.parts + r, row)
            here = take(rec, part * self.sl + spot % self.sl)
            value = here if value is None else jnp.where(spot // self.sl == r, here, value)
        return value

    def place(self, terms, shift, sub):
        lane = self.lane()
        part, spot = lane // self.sl % 2, lane % self.sl
        if self.per:
            value = take(terms, shift + part * TILE + spot % TILE)
            keep = spot // TILE == sub
        else:
            value = take(terms, shift + part * TILE + sub * self.sl + spot)
            keep = lane < 2 * self.sl
        return jnp.where(keep, value, 0.0)

    def spread(self, me, tile, terms, shift, own_ref, sib_ref):
        if self.per:
            device = tile // self.per
            spots = [(device, tile - device * self.per)]
        else:
            spots = [(tile * self.parts + r, r) for r in range(self.parts)]
        for device, sub in spots:
            value = self.place(terms, shift, sub)
            same, slot = self.owner(me, device)
            own_ref[slot] = own_ref[slot] + jnp.where(same, value, 0.0)
            sib_ref[slot] = sib_ref[slot] + jnp.where(same, 0.0, value)

    def record_of(self, raw_ref):
        pieces = [raw_ref[0, 0], raw_ref[0, 1]]
        if 2 * self.sl < LANES:
            pieces.append(jnp.zeros((self.k, LANES - 2 * self.sl), jnp.float32))
        return jnp.concatenate(pieces, axis=1)


def take(value, lanes):
    return jnp.take_along_axis(value, lanes, axis=1, mode="promise_in_bounds")


def merge(low, first, second, shift, axis):
    size = first.shape[axis]
    if 2 * shift == size:
        mixed = jnp.where(low, second, first)
        return jnp.where(low, first, second) + pltpu.roll(mixed, shift, axis)
    up = first + pltpu.roll(first, size - shift, axis)
    down = second + pltpu.roll(second, shift, axis)
    return jnp.where(low, up, down)


def merge_all(items, shifts, axis):
    index = lax.broadcasted_iota(jnp.int32, items[0].shape, axis)
    for shift in shifts:
        half = len(items) // 2
        low = (index & shift) == 0
        items = [merge(low, items[i], items[i + half], shift, axis) for i in range(half)]
    return items


def eights(value):
    return [value[8 * i : 8 * i + 8] for i in range(value.shape[0] // 8)]


def pack_kernel(plan, tiles_hbm, counts_hbm, gains_hbm, targets_hbm, mult_hbm, out_ref, meta_ref, mrec_ref, *scratch):
    bufs, sems = scratch[:-1], scratch[-1]
    copies = [
        pltpu.make_async_copy(src, dst, sems.at[i])
        for i, (src, dst) in enumerate(zip((gains_hbm, targets_hbm, mult_hbm, tiles_hbm, counts_hbm), bufs))
    ]
    for copy in copies:
        copy.start()
    for copy in copies:
        copy.wait()
    gains_ref, targets_ref, mult_ref, tiles_ref, counts_ref = bufs
    k = plan.k
    gain = plan.record_of(gains_ref)
    target = plan.record_of(targets_ref)
    mult = plan.record_of(mult_ref)
    out_ref[:k] = gain
    out_ref[k : 2 * k] = gain - penalty * (gain - target + mult)
    mrec_ref[...] = mult
    lane = plan.lane(8)
    sub = lax.broadcasted_iota(jnp.int32, (8, LANES), 0)
    meta = jnp.zeros((8, LANES), jnp.int32)
    for base in range(0, plan.blocks, 8):
        rows = jnp.zeros((8, LANES), jnp.int32)
        for n in range(base, min(base + 8, plan.blocks)):
            ids = jnp.where(lane < 2 * TILE, tiles_ref[n, 0], tiles_ref[n, 1])
            rows = jnp.where(sub == n - base, ids, rows)
            for j, number in enumerate((tiles_ref[n, 0], tiles_ref[n, 1], counts_ref[n])):
                meta = jnp.where(lane == 3 * n + j, number, meta)
        out_ref[2 * k + base : 2 * k + base + 8] = rows.astype(jnp.float32)
    meta_ref[...] = meta


def load_kernel(plan, vis_hbm, coh_hbm, vis_ref, coh_ref, vis_buf, coh_buf, sems):
    halves = 2
    cells = plan.cells // halves
    copies = []
    for n in range(plan.blocks):
        for h in range(halves):
            lanes = pl.ds(h * cells, cells)
            copies.append(
                pltpu.make_async_copy(
                    coh_hbm.at[0, n, :, :, :, lanes],
                    coh_buf.at[n, :, :, :, lanes],
                    sems.at[n * halves + h],
                )
            )
    last = pltpu.make_async_copy(vis_hbm.at[0], vis_buf, sems.at[plan.blocks * halves])
    for copy in copies:
        copy.start()
    last.start()
    for n in range(plan.blocks):
        for h in range(halves):
            copies[n * halves + h].wait()

            def convert(t, carry, n=n, h=h):
                lanes = pl.ds(h * cells, cells)
                coh_ref[n, t, :, :, lanes] = coh_buf[n, t, :, :, lanes].astype(jnp.float32)
                return carry

            lax.fori_loop(0, plan.times, convert, 0)
    last.wait()
    for n in range(plan.blocks):
        for part in range(2):
            vis_ref[n, part] = vis_buf[n, :, part, :]


def block_gradients(plan, meta_ref, tile_gains, vis_ref, coh_ref, right_ref, left_ref, second_ref, first_ref):
    k, times, steps = plan.k, plan.times, plan.steps
    lane_k = plan.lane()
    lane = plan.lane(8)
    sample = lax.broadcasted_iota(jnp.int32, (8, LANES), 0)
    for n, (left, right) in enumerate(tile_gains):
        left_ref[n] = left
        right_ref[n, 0] = take(right, lane_k % TILE)
        right_ref[n, 1] = take(right, TILE + lane_k % TILE)
        second_ref[n] = jnp.zeros((2, k, LANES), jnp.float32)

    def lefts(n, index):
        left = left_ref[n]
        spot = index * GROUP + lane_k // TILE
        return take(left, spot), take(left, TILE + spot)

    def where_is(q):
        n = q // steps
        index = q - n * steps
        return n, index, pl.ds(pl.multiple_of(index * LANES, LANES), LANES)

    def residual(q):
        n, index, lanes = where_is(q)
        lr, li = lefts(n, index)
        rr, ri = right_ref[n, 0], right_ref[n, 1]
        pr = lr * rr + li * ri
        pi = li * rr - lr * ri
        reals, imags = [], []
        for t in range(times):
            cr = coh_ref[n, t, 0, :, lanes]
            ci = coh_ref[n, t, 1, :, lanes]
            reals.append(sum(eights(pr * cr - pi * ci)))
            imags.append(sum(eights(pr * ci + pi * cr)))
        none = jnp.zeros((8, LANES), jnp.float32)
        reals += [none] * (8 - times)
        imags += [none] * (8 - times)
        (mr,) = merge_all(reals, (4, 2, 1), 0)
        (mi,) = merge_all(imags, (4, 2, 1), 0)
        upper = index * GROUP + lane // TILE - lane % TILE
        differ = meta_ref[0, 3 * n] != meta_ref[0, 3 * n + 1]
        bound = jnp.where(differ, steps * LANES, 0)
        keep = (upper < bound) & (sample < meta_ref[0, 3 * n + 2])
        er = jnp.where(keep, vis_ref[n, 0, :, lanes] - mr, 0.0)
        ei = jnp.where(keep, vis_ref[n, 1, :, lanes] - mi, 0.0)
        return er, ei

    def gradient(q, errors):
        er, ei = errors
        n, index, lanes = where_is(q)
        acc_re = acc_im = None
        for t in range(times):
            cr = coh_ref[n, t, 0, :, lanes]
            ci = coh_ref[n, t, 1, :, lanes]
            r = jnp.broadcast_to(er[t : t + 1], (k, LANES))
            i = jnp.broadcast_to(ei[t : t + 1], (k, LANES))
            re = r * cr + i * ci
            im = i * cr - r * ci
            acc_re = re if acc_re is None else acc_re + re
            acc_im = im if acc_im is None else acc_im + im
        lr, li = lefts(n, index)
        rr, ri = right_ref[n, 0], right_ref[n, 1]
        second_ref[n, 0] = second_ref[n, 0] + (acc_re * lr + acc_im * li)
        second_ref[n, 1] = second_ref[n, 1] + (acc_re * li - acc_im * lr)
        parts = eights(acc_re * rr - acc_im * ri) + eights(acc_re * ri + acc_im * rr)
        (total,) = merge_all(parts, (16, 8, 4), 1)
        for shift in (2, 1):
            (total,) = merge_all([total, total], (shift,), 1)
        first_ref[n, index] = total

    def step(q, errors):
        following = residual(q + 1)
        gradient(q, errors)
        return following

    final = plan.blocks * steps - 1
    gradient(final, lax.fori_loop(0, final, step, residual(0)))

    results = []
    for n in range(plan.blocks):
        packed = []
        for base in range(0, steps, 4):
            value = first_ref[n, base]
            for r in range(1, 4):
                value = jnp.where(lane % 4 == r, first_ref[n, base + r], value)
            packed.append(value)
        seconds = merge_all(eights(second_ref[n, 0]) + eights(second_ref[n, 1]), (64, 32), 1)
        part, spot = lane // TILE % 2, lane % TILE
        rows = []
        for group in range(k // 8):
            source = spot % GROUP * TILE + part * 16 + group * 4 + spot // GROUP % 4
            value = take(packed[0], source)
            for h in range(1, len(packed)):
                value = jnp.where(spot // 16 == h, take(packed[h], source), value)
            other = take(seconds[group % 2], part * 64 + group // 2 * TILE + spot)
            rows.append(jnp.where(lane < 2 * TILE, value, other))
        results.append(jnp.concatenate(rows, axis=0))
    return results


def first_kernel(plan, meta_ref, own_ref, sib_ref, vis_ref, coh_ref, out_ref, *scratch):
    me = lax.axis_index("pair")
    tile_gains = [
        [plan.fetch(me, own_ref, sib_ref, meta_ref[0, 3 * n + side], 0) for side in range(2)]
        for n in range(plan.blocks)
    ]
    for n, terms in enumerate(block_gradients(plan, meta_ref, tile_gains, vis_ref, coh_ref, *scratch)):
        out_ref[n] = terms


def second_kernel(
    plan, step_size, meta_ref, own_ref, sib_ref, term_own_ref, term_sib_ref, mult_ref, vis_ref, coh_ref,
    part_own_ref, part_sib_ref, rest_ref, *scratch,
):
    k = plan.k
    me = lax.axis_index("pair")
    wanted = [meta_ref[0, 3 * n + side] for n in range(plan.blocks) for side in range(2)]
    if plan.per:
        wanted += [me * plan.per + s for s in range(plan.per)]
    else:
        wanted += [me // plan.parts]
    labels = [t.astype(jnp.float32) for t in wanted]

    def gather(slot, sums):
        for pay_ref, term_ref in ((own_ref, term_own_ref), (sib_ref, term_sib_ref)):
            ids_all = pay_ref[slot, 2 * k : plan.rows, :]
            for n in range(plan.blocks):
                ids = ids_all[n : n + 1]
                terms = term_ref[slot, n]
                sums = [s + jnp.where(ids == label, terms, 0.0) for s, label in zip(sums, labels)]
        return sums

    sums = [jnp.zeros((k, LANES), jnp.float32) for _ in wanted]
    if plan.zn <= 4:
        for slot in range(plan.zn):
            sums = gather(slot, sums)
    else:
        sums = lax.fori_loop(0, plan.zn, gather, sums)
    sums = [s + pltpu.roll(s, LANES // 2, 1) for s in sums]

    tile_gains = [
        [
            plan.fetch(me, own_ref, sib_ref, wanted[2 * n + side], k) + step_size * sums[2 * n + side]
            for side in range(2)
        ]
        for n in range(plan.blocks)
    ]

    mine = sums[2 * plan.blocks :]
    if plan.per:
        own_sum = sum(plan.place(value, 0, s) for s, value in enumerate(mine))
    else:
        own_sum = plan.place(mine[0], 0, me % plan.parts)
    start = own_ref[0, :k, :]
    base = own_ref[0, k : 2 * k, :]
    pull = base - (1.0 - penalty) * start
    rest = (1.0 - penalty) * (base + step_size * own_sum) + pull
    rest_ref[0] = rest
    rest_ref[1] = rest + mult_ref[...]

    part_own_ref[...] = jnp.zeros_like(part_own_ref)
    part_sib_ref[...] = jnp.zeros_like(part_sib_ref)
    for n, terms in enumerate(block_gradients(plan, meta_ref, tile_gains, vis_ref, coh_ref, *scratch)):
        for side in range(2):
            plan.spread(me, meta_ref[0, 3 * n + side], terms, side * 2 * TILE, part_own_ref, part_sib_ref)


def fit_kernel(plan, fit, gain_ref, own_ref, *refs):
    others, (gain_out, target_out, mult_out) = refs[:-3], refs[-3:]
    sl = plan.sl
    band = lax.axis_index("band")
    total = None
    for m, ref in enumerate((own_ref,) + tuple(others)):
        factor = jnp.float32(0.0)
        for f in range(fit.shape[0]):
            factor = jnp.where(band == f, jnp.float32(fit[f, f ^ m]), factor)
        value = factor * ref[...]
        total = value if total is None else total + value
    change = own_ref[...] - total
    gain = gain_ref[...]
    for part in range(2):
        lanes = slice(part * sl, (part + 1) * sl)
        gain_out[0, part] = gain[:, lanes]
        target_out[0, part] = total[:, lanes]
        mult_out[0, part] = change[:, lanes]


def exchange(value, axis, size, mask):
    return lax.ppermute(value, axis, [(i, i ^ mask) for i in range(size)])


def local(visibilities, coherencies, block_tiles, sample_counts, gains, targets, multipliers):
    pairs = lax.axis_size("pair")
    bands = lax.axis_size("band")
    _, blocks, times, _, directions, cells = coherencies.shape
    stations = gains.shape[3]
    plan = Plan(directions, stations, pairs, blocks, times, cells)
    k, zn = plan.k, plan.zn
    tile_count = stations * pairs // TILE
    step_size = 0.25 * tile_count * k / (times * TILE * blocks * pairs)

    smem = pl.BlockSpec(memory_space=pltpu.SMEM)
    vmem = pl.BlockSpec(memory_space=pltpu.VMEM)
    hbm = pl.BlockSpec(memory_space=pltpu.HBM)
    stay = lambda value: pltpu.with_memory_space_constraint(value, pltpu.HBM)
    f32 = lambda *shape: jax.ShapeDtypeStruct(shape, jnp.float32)
    scratch = [
        pltpu.VMEM((blocks, 2, k, LANES), jnp.float32),
        pltpu.VMEM((blocks, k, LANES), jnp.float32),
        pltpu.VMEM((blocks, 2, k, LANES), jnp.float32),
        pltpu.VMEM((blocks, plan.steps, 8, LANES), jnp.float32),
    ]
    params = pltpu.CompilerParams(vmem_limit_bytes=16 << 20)

    payload, meta, mult_rec = pl.pallas_call(
        lambda *refs: pack_kernel(plan, *refs),
        name="pack",
        in_specs=[hbm] * 5,
        out_specs=[vmem] * 3,
        out_shape=[f32(plan.rows, LANES), jax.ShapeDtypeStruct((8, LANES), jnp.int32), f32(k, LANES)],
        scratch_shapes=[pltpu.VMEM(gains.shape, jnp.float32)] * 3
        + [
            pltpu.SMEM(block_tiles.shape, jnp.int32),
            pltpu.SMEM(sample_counts.shape, jnp.int32),
            pltpu.SemaphoreType.DMA((5,)),
        ],
        compiler_params=params,
    )(*map(stay, (block_tiles, sample_counts, gains, targets, multipliers)))

    vis, coh = pl.pallas_call(
        lambda *refs: load_kernel(plan, *refs),
        name="load",
        in_specs=[hbm] * 2,
        out_specs=[vmem] * 2,
        out_shape=[f32(blocks, 2, times, cells), f32(blocks, times, 2, k, cells)],
        scratch_shapes=[
            pltpu.VMEM((blocks, times, 2, cells), jnp.float32),
            pltpu.VMEM((blocks, times, 2, k, cells), jnp.bfloat16),
            pltpu.SemaphoreType.DMA((2 * blocks + 1,)),
        ],
        compiler_params=params,
    )(stay(visibilities), stay(coherencies))

    def gather(value):
        parts = [value] + [exchange(value, "pair", pairs, 2 * m) for m in range(1, zn)]
        own = jnp.stack(parts)
        return own, exchange(own, "pair", pairs, 1)

    own, sib = gather(payload)

    terms = pl.pallas_call(
        lambda *refs: first_kernel(plan, *refs),
        name="first",
        in_specs=[smem, vmem, vmem, vmem, vmem],
        out_specs=vmem,
        out_shape=f32(blocks, k, LANES),
        scratch_shapes=scratch,
        compiler_params=params,
    )(meta, own, sib, vis, coh)

    term_own, term_sib = gather(terms)
    part_own, part_sib, rest = pl.pallas_call(
        lambda *refs: second_kernel(plan, step_size, *refs),
        name="second",
        in_specs=[smem] + [vmem] * 7,
        out_specs=[vmem, vmem, vmem],
        out_shape=[f32(zn, k, LANES), f32(zn, k, LANES), f32(2, k, LANES)],
        scratch_shapes=scratch,
        compiler_params=params,
    )(meta, own, sib, term_own, term_sib, mult_rec, vis, coh)

    crossed = exchange(part_sib, "pair", pairs, 1)
    total = part_own[0] + crossed[0]
    for m in range(1, zn):
        total = total + exchange(part_own[m] + crossed[m], "pair", pairs, 2 * m)
    new_gain = rest[0] + step_size * total
    summed = rest[1] + step_size * total

    others = [exchange(summed, "band", bands, m) for m in range(1, bands)]
    shape = f32(*gains.shape)
    return pl.pallas_call(
        lambda *refs: fit_kernel(plan, fit_matrix(bands, P_SIZE), *refs),
        name="fit",
        in_specs=[vmem] * (2 + len(others)),
        out_specs=[vmem] * 3,
        out_shape=[shape] * 3,
        compiler_params=params,
    )(new_gain, summed, *others)


def solution(mesh):
    placed = (
        P("band", "pair", None, None, None),
        P("band", "pair", None, None, None, None),
        P("pair", None),
        P("pair"),
        P("band", None, None, "pair"),
        P("band", None, None, "pair"),
        P("band", None, None, "pair"),
    )
    return jax.shard_map(
        local,
        mesh=mesh,
        in_specs=placed,
        out_specs=(
            P("band", None, None, "pair"),
            P("band", None, None, "pair"),
            P("band", None, None, "pair"),
        ),
        check_vma=False,
    )
```

```python
import math

import jax
import jax.numpy as jnp
import numpy as np
from jax import lax
from jax.experimental import pallas as pl
from jax.experimental.pallas import tpu as pltpu
from jax.sharding import PartitionSpec as P


P_SIZE = 8
TILE = 32
LANES = 128
GROUP = LANES // TILE

ridge = 0.05
penalty = 0.25


def fit_matrix(freq_count, term_count):
    positions = (np.arange(freq_count) + 0.5) / freq_count
    basis = np.stack(
        [
            math.comb(term_count - 1, degree)
            * positions**degree
            * (1.0 - positions) ** (term_count - 1 - degree)
            for degree in range(term_count)
        ],
        axis=1,
    )
    normal = basis.T @ basis + ridge * np.eye(term_count)
    factor = np.linalg.cholesky(normal)
    half = np.linalg.solve(factor, basis.T)
    return half.T @ half


class Plan:
    def __init__(self, directions, stations, pairs, blocks, times, cells):
        self.k = directions
        self.sl = stations
        self.zn = pairs // 2
        self.blocks = blocks
        self.times = times
        self.cells = cells
        self.steps = cells // LANES
        self.per = stations // TILE
        self.parts = 1 if self.per else TILE // stations
        self.rows = 2 * directions + 8 * ((blocks + 7) // 8)
        assert 2 * stations <= LANES and directions == 32 and times <= 8 and self.steps == 8

    def lane(self, rows=None):
        return lax.broadcasted_iota(jnp.int32, (self.k if rows is None else rows, LANES), 1)

    def owner(self, me, device):
        return (device % 2) == (me % 2), (device // 2) ^ (me // 2)

    def record(self, me, own_ref, sib_ref, device, row):
        same, slot = self.owner(me, device)
        own = own_ref[slot, row : row + self.k, :]
        sib = sib_ref[slot, row : row + self.k, :]
        return jnp.where(same, own, sib)

    def fetch(self, me, own_ref, sib_ref, tile, row):
        lane = self.lane()
        part, spot = lane // TILE % 2, lane % TILE
        if self.per:
            device = tile // self.per
            sub = tile - device * self.per
            rec = self.record(me, own_ref, sib_ref, device, row)
            return take(rec, part * self.sl + sub * TILE + spot)
        value = None
        for r in range(self.parts):
            rec = self.record(me, own_ref, sib_ref, tile * self.parts + r, row)
            here = take(rec, part * self.sl + spot % self.sl)
            value = here if value is None else jnp.where(spot // self.sl == r, here, value)
        return value

    def place(self, terms, shift, sub):
        lane = self.lane()
        part, spot = lane // self.sl % 2, lane % self.sl
        if self.per:
            value = take(terms, shift + part * TILE + spot % TILE)
            keep = spot // TILE == sub
        else:
            value = take(terms, shift + part * TILE + sub * self.sl + spot)
            keep = lane < 2 * self.sl
        return jnp.where(keep, value, 0.0)

    def spread(self, me, tile, terms, shift, own_ref, sib_ref):
        if self.per:
            device = tile // self.per
            spots = [(device, tile - device * self.per)]
        else:
            spots = [(tile * self.parts + r, r) for r in range(self.parts)]
        for device, sub in spots:
            value = self.place(terms, shift, sub)
            same, slot = self.owner(me, device)
            own_ref[slot] = own_ref[slot] + jnp.where(same, value, 0.0)
            sib_ref[slot] = sib_ref[slot] + jnp.where(same, 0.0, value)

    def record_of(self, raw_ref):
        pieces = [raw_ref[0, 0], raw_ref[0, 1]]
        if 2 * self.sl < LANES:
            pieces.append(jnp.zeros((self.k, LANES - 2 * self.sl), jnp.float32))
        return jnp.concatenate(pieces, axis=1)


def take(value, lanes):
    return jnp.take_along_axis(value, lanes, axis=1, mode="promise_in_bounds")


def merge(low, first, second, shift, axis):
    size = first.shape[axis]
    if axis == 1 or 2 * shift == size:
        mixed = jnp.where(low, second, first)
        if 2 * shift == size:
            mixed = pltpu.roll(mixed, shift, axis)
        else:
            mixed = take(mixed, lax.broadcasted_iota(jnp.int32, mixed.shape, 1) ^ shift)
        return jnp.where(low, first, second) + mixed
    up = first + pltpu.roll(first, size - shift, axis)
    down = second + pltpu.roll(second, shift, axis)
    return jnp.where(low, up, down)


def merge_all(items, shifts, axis):
    index = lax.broadcasted_iota(jnp.int32, items[0].shape, axis)
    for shift in shifts:
        half = len(items) // 2
        low = (index & shift) == 0
        items = [merge(low, items[i], items[i + half], shift, axis) for i in range(half)]
    return items


def eights(value):
    return [value[8 * i : 8 * i + 8] for i in range(value.shape[0] // 8)]


def pack_kernel(plan, tiles_hbm, counts_hbm, gains_hbm, targets_hbm, mult_hbm, out_ref, meta_ref, mrec_ref, *scratch):
    bufs, sems = scratch[:-1], scratch[-1]
    copies = [
        pltpu.make_async_copy(src, dst, sems.at[i])
        for i, (src, dst) in enumerate(zip((gains_hbm, targets_hbm, mult_hbm, tiles_hbm, counts_hbm), bufs))
    ]
    for copy in copies:
        copy.start()
    for copy in copies:
        copy.wait()
    gains_ref, targets_ref, mult_ref, tiles_ref, counts_ref = bufs
    k = plan.k
    gain = plan.record_of(gains_ref)
    target = plan.record_of(targets_ref)
    mult = plan.record_of(mult_ref)
    out_ref[:k] = gain
    out_ref[k : 2 * k] = gain - penalty * (gain - target + mult)
    mrec_ref[...] = mult
    lane = plan.lane(8)
    sub = lax.broadcasted_iota(jnp.int32, (8, LANES), 0)
    meta = jnp.zeros((8, LANES), jnp.int32)
    for base in range(0, plan.blocks, 8):
        rows = jnp.zeros((8, LANES), jnp.int32)
        for n in range(base, min(base + 8, plan.blocks)):
            ids = jnp.where(lane < 2 * TILE, tiles_ref[n, 0], tiles_ref[n, 1])
            rows = jnp.where(sub == n - base, ids, rows)
            for j, number in enumerate((tiles_ref[n, 0], tiles_ref[n, 1], counts_ref[n])):
                meta = jnp.where(lane == 3 * n + j, number, meta)
        out_ref[2 * k + base : 2 * k + base + 8] = rows.astype(jnp.float32)
    meta_ref[...] = meta


def load_kernel(plan, vis_hbm, coh_hbm, vis_ref, coh_ref, vis_buf, coh_buf, sems):
    halves = 2
    cells = plan.cells // halves
    copies = []
    for n in range(plan.blocks):
        for h in range(halves):
            lanes = pl.ds(h * cells, cells)
            copies.append(
                pltpu.make_async_copy(
                    coh_hbm.at[0, n, :, :, :, lanes],
                    coh_buf.at[n, :, :, :, lanes],
                    sems.at[n * halves + h],
                )
            )
    last = pltpu.make_async_copy(vis_hbm.at[0], vis_buf, sems.at[plan.blocks * halves])
    for copy in copies:
        copy.start()
    last.start()
    for n in range(plan.blocks):
        for h in range(halves):
            copies[n * halves + h].wait()

            def convert(t, carry, n=n, h=h):
                lanes = pl.ds(h * cells, cells)
                coh_ref[n, t, :, :, lanes] = coh_buf[n, t, :, :, lanes].astype(jnp.float32)
                return carry

            lax.fori_loop(0, plan.times, convert, 0)
    last.wait()
    for n in range(plan.blocks):
        for part in range(2):
            vis_ref[n, part] = vis_buf[n, :, part, :]


def block_gradients(plan, meta_ref, tile_gains, vis_ref, coh_ref, right_ref, left_ref, wide_ref, second_ref, first_ref):
    k, times, steps = plan.k, plan.times, plan.steps
    lane_k = plan.lane()
    lane = plan.lane(8)
    sample = lax.broadcasted_iota(jnp.int32, (8, LANES), 0)
    for n, (left, right) in enumerate(tile_gains):
        left_ref[n] = left
        right_ref[n, 0] = take(right, lane_k % TILE)
        right_ref[n, 1] = take(right, TILE + lane_k % TILE)
        second_ref[n] = jnp.zeros((2, k, LANES), jnp.float32)

    def lefts(q):
        n, index, _ = where_is(q)
        left = left_ref[n]
        spot = index * GROUP + lane_k // TILE
        wide_ref[n, index, 0] = take(left, spot)
        wide_ref[n, index, 1] = take(left, TILE + spot)

    def where_is(q):
        n = q // steps
        index = q - n * steps
        return n, index, pl.ds(pl.multiple_of(index * LANES, LANES), LANES)

    def residual(q):
        n, index, lanes = where_is(q)
        lr, li = wide_ref[n, index, 0], wide_ref[n, index, 1]
        rr, ri = right_ref[n, 0], right_ref[n, 1]
        pr = lr * rr + li * ri
        pi = li * rr - lr * ri
        reals, imags = [], []
        for t in range(times):
            cr = coh_ref[n, t, 0, :, lanes]
            ci = coh_ref[n, t, 1, :, lanes]
            reals.append(sum(eights(pr * cr - pi * ci)))
            imags.append(sum(eights(pr * ci + pi * cr)))
        none = jnp.zeros((8, LANES), jnp.float32)
        reals += [none] * (8 - times)
        imags += [none] * (8 - times)
        (mr,) = merge_all(reals, (4, 2, 1), 0)
        (mi,) = merge_all(imags, (4, 2, 1), 0)
        upper = index * GROUP + lane // TILE - lane % TILE
        differ = meta_ref[0, 3 * n] != meta_ref[0, 3 * n + 1]
        bound = jnp.where(differ, steps * LANES, 0)
        keep = (upper < bound) & (sample < meta_ref[0, 3 * n + 2])
        er = jnp.where(keep, vis_ref[n, 0, :, lanes] - mr, 0.0)
        ei = jnp.where(keep, vis_ref[n, 1, :, lanes] - mi, 0.0)
        return er, ei

    def gradient(q, errors):
        er, ei = errors
        n, index, lanes = where_is(q)
        acc_re = acc_im = None
        for t in range(times):
            cr = coh_ref[n, t, 0, :, lanes]
            ci = coh_ref[n, t, 1, :, lanes]
            r = jnp.broadcast_to(er[t : t + 1], (k, LANES))
            i = jnp.broadcast_to(ei[t : t + 1], (k, LANES))
            re = r * cr + i * ci
            im = i * cr - r * ci
            acc_re = re if acc_re is None else acc_re + re
            acc_im = im if acc_im is None else acc_im + im
        lr, li = wide_ref[n, index, 0], wide_ref[n, index, 1]
        rr, ri = right_ref[n, 0], right_ref[n, 1]
        second_ref[n, 0] = second_ref[n, 0] + (acc_re * lr + acc_im * li)
        second_ref[n, 1] = second_ref[n, 1] + (acc_re * li - acc_im * lr)
        first_ref[n, index, 0] = acc_re * rr - acc_im * ri
        first_ref[n, index, 1] = acc_re * ri + acc_im * rr

    final = plan.blocks * steps - 1

    def step(q, errors):
        lefts(jnp.minimum(q + 2, final))
        following = residual(q + 1)
        gradient(q, errors)
        return following

    lefts(0)
    lefts(1)
    gradient(final, lax.fori_loop(0, final, step, residual(0)))

    results = []
    for n in range(plan.blocks):
        items = [
            first_ref[n, 4 * h + r, part, 8 * group : 8 * group + 8, :]
            for part in range(2)
            for group in range(k // 8)
            for r in range(4)
            for h in range(steps // 4)
        ]
        packed = merge_all(items, (16, 8, 4, 2, 1), 1)
        seconds = merge_all(eights(second_ref[n, 0]) + eights(second_ref[n, 1]), (64, 32), 1)
        part, spot = lane // TILE % 2, lane % TILE
        rows = []
        for group in range(k // 8):
            source = spot % GROUP * TILE + part * 16 + group * 4 + spot // GROUP % 4
            value = take(packed[0], source)
            for h in range(1, len(packed)):
                value = jnp.where(spot // 16 == h, take(packed[h], source), value)
            other = take(seconds[group % 2], part * 64 + group // 2 * TILE + spot)
            rows.append(jnp.where(lane < 2 * TILE, value, other))
        results.append(jnp.concatenate(rows, axis=0))
    return results


def first_kernel(plan, meta_ref, own_ref, sib_ref, vis_ref, coh_ref, out_ref, *scratch):
    me = lax.axis_index("pair")
    tile_gains = [
        [plan.fetch(me, own_ref, sib_ref, meta_ref[0, 3 * n + side], 0) for side in range(2)]
        for n in range(plan.blocks)
    ]
    for n, terms in enumerate(block_gradients(plan, meta_ref, tile_gains, vis_ref, coh_ref, *scratch)):
        out_ref[n] = terms


def second_kernel(
    plan, step_size, meta_ref, own_ref, sib_ref, term_own_ref, term_sib_ref, mult_ref, vis_ref, coh_ref,
    part_own_ref, part_sib_ref, rest_ref, *scratch,
):
    k = plan.k
    me = lax.axis_index("pair")
    wanted = [meta_ref[0, 3 * n + side] for n in range(plan.blocks) for side in range(2)]
    if plan.per:
        wanted += [me * plan.per + s for s in range(plan.per)]
    else:
        wanted += [me // plan.parts]
    labels = [t.astype(jnp.float32) for t in wanted]

    def gather(slot, sums):
        for pay_ref, term_ref in ((own_ref, term_own_ref), (sib_ref, term_sib_ref)):
            ids_all = pay_ref[slot, 2 * k : plan.rows, :]
            for n in range(plan.blocks):
                ids = ids_all[n : n + 1]
                terms = term_ref[slot, n]
                sums = [s + jnp.where(ids == label, terms, 0.0) for s, label in zip(sums, labels)]
        return sums

    sums = [jnp.zeros((k, LANES), jnp.float32) for _ in wanted]
    if plan.zn <= 4:
        for slot in range(plan.zn):
            sums = gather(slot, sums)
    else:
        sums = lax.fori_loop(0, plan.zn, gather, sums)
    sums = [s + pltpu.roll(s, LANES // 2, 1) for s in sums]

    tile_gains = [
        [
            plan.fetch(me, own_ref, sib_ref, wanted[2 * n + side], k) + step_size * sums[2 * n + side]
            for side in range(2)
        ]
        for n in range(plan.blocks)
    ]

    mine = sums[2 * plan.blocks :]
    if plan.per:
        own_sum = sum(plan.place(value, 0, s) for s, value in enumerate(mine))
    else:
        own_sum = plan.place(mine[0], 0, me % plan.parts)
    start = own_ref[0, :k, :]
    base = own_ref[0, k : 2 * k, :]
    pull = base - (1.0 - penalty) * start
    rest = (1.0 - penalty) * (base + step_size * own_sum) + pull
    rest_ref[0] = rest
    rest_ref[1] = rest + mult_ref[...]

    part_own_ref[...] = jnp.zeros_like(part_own_ref)
    part_sib_ref[...] = jnp.zeros_like(part_sib_ref)
    for n, terms in enumerate(block_gradients(plan, meta_ref, tile_gains, vis_ref, coh_ref, *scratch)):
        for side in range(2):
            plan.spread(me, meta_ref[0, 3 * n + side], terms, side * 2 * TILE, part_own_ref, part_sib_ref)


def fit_kernel(plan, fit, gain_ref, own_ref, *refs):
    others, (gain_out, target_out, mult_out) = refs[:-3], refs[-3:]
    sl = plan.sl
    band = lax.axis_index("band")
    total = None
    for m, ref in enumerate((own_ref,) + tuple(others)):
        factor = jnp.float32(0.0)
        for f in range(fit.shape[0]):
            factor = jnp.where(band == f, jnp.float32(fit[f, f ^ m]), factor)
        value = factor * ref[...]
        total = value if total is None else total + value
    change = own_ref[...] - total
    gain = gain_ref[...]
    for part in range(2):
        lanes = slice(part * sl, (part + 1) * sl)
        gain_out[0, part] = gain[:, lanes]
        target_out[0, part] = total[:, lanes]
        mult_out[0, part] = change[:, lanes]


def exchange(value, axis, size, mask):
    return lax.ppermute(value, axis, [(i, i ^ mask) for i in range(size)])


def local(visibilities, coherencies, block_tiles, sample_counts, gains, targets, multipliers):
    pairs = lax.axis_size("pair")
    bands = lax.axis_size("band")
    _, blocks, times, _, directions, cells = coherencies.shape
    stations = gains.shape[3]
    plan = Plan(directions, stations, pairs, blocks, times, cells)
    k, zn = plan.k, plan.zn
    tile_count = stations * pairs // TILE
    step_size = 0.25 * tile_count * k / (times * TILE * blocks * pairs)

    smem = pl.BlockSpec(memory_space=pltpu.SMEM)
    vmem = pl.BlockSpec(memory_space=pltpu.VMEM)
    hbm = pl.BlockSpec(memory_space=pltpu.HBM)
    stay = lambda value: pltpu.with_memory_space_constraint(value, pltpu.HBM)
    f32 = lambda *shape: jax.ShapeDtypeStruct(shape, jnp.float32)
    scratch = [
        pltpu.VMEM((blocks, 2, k, LANES), jnp.float32),
        pltpu.VMEM((blocks, k, LANES), jnp.float32),
        pltpu.VMEM((blocks, plan.steps, 2, k, LANES), jnp.float32),
        pltpu.VMEM((blocks, 2, k, LANES), jnp.float32),
        pltpu.VMEM((blocks, plan.steps, 2, k, LANES), jnp.float32),
    ]
    params = pltpu.CompilerParams(vmem_limit_bytes=16 << 20)

    payload, meta, mult_rec = pl.pallas_call(
        lambda *refs: pack_kernel(plan, *refs),
        name="pack",
        in_specs=[hbm] * 5,
        out_specs=[vmem] * 3,
        out_shape=[f32(plan.rows, LANES), jax.ShapeDtypeStruct((8, LANES), jnp.int32), f32(k, LANES)],
        scratch_shapes=[pltpu.VMEM(gains.shape, jnp.float32)] * 3
        + [
            pltpu.SMEM(block_tiles.shape, jnp.int32),
            pltpu.SMEM(sample_counts.shape, jnp.int32),
            pltpu.SemaphoreType.DMA((5,)),
        ],
        compiler_params=params,
    )(*map(stay, (block_tiles, sample_counts, gains, targets, multipliers)))

    vis, coh = pl.pallas_call(
        lambda *refs: load_kernel(plan, *refs),
        name="load",
        in_specs=[hbm] * 2,
        out_specs=[vmem] * 2,
        out_shape=[f32(blocks, 2, times, cells), f32(blocks, times, 2, k, cells)],
        scratch_shapes=[
            pltpu.VMEM((blocks, times, 2, cells), jnp.float32),
            pltpu.VMEM((blocks, times, 2, k, cells), jnp.bfloat16),
            pltpu.SemaphoreType.DMA((2 * blocks + 1,)),
        ],
        compiler_params=params,
    )(stay(visibilities), stay(coherencies))

    def gather(value):
        parts = [value] + [exchange(value, "pair", pairs, 2 * m) for m in range(1, zn)]
        own = jnp.stack(parts)
        return own, exchange(own, "pair", pairs, 1)

    own, sib = gather(payload)

    terms = pl.pallas_call(
        lambda *refs: first_kernel(plan, *refs),
        name="first",
        in_specs=[smem, vmem, vmem, vmem, vmem],
        out_specs=vmem,
        out_shape=f32(blocks, k, LANES),
        scratch_shapes=scratch,
        compiler_params=params,
    )(meta, own, sib, vis, coh)

    term_own, term_sib = gather(terms)
    part_own, part_sib, rest = pl.pallas_call(
        lambda *refs: second_kernel(plan, step_size, *refs),
        name="second",
        in_specs=[smem] + [vmem] * 7,
        out_specs=[vmem, vmem, vmem],
        out_shape=[f32(zn, k, LANES), f32(zn, k, LANES), f32(2, k, LANES)],
        scratch_shapes=scratch,
        compiler_params=params,
    )(meta, own, sib, term_own, term_sib, mult_rec, vis, coh)

    crossed = exchange(part_sib, "pair", pairs, 1)
    total = part_own[0] + crossed[0]
    for m in range(1, zn):
        total = total + exchange(part_own[m] + crossed[m], "pair", pairs, 2 * m)
    new_gain = rest[0] + step_size * total
    summed = rest[1] + step_size * total

    others = [exchange(summed, "band", bands, m) for m in range(1, bands)]
    shape = f32(*gains.shape)
    return pl.pallas_call(
        lambda *refs: fit_kernel(plan, fit_matrix(bands, P_SIZE), *refs),
        name="fit",
        in_specs=[vmem] * (2 + len(others)),
        out_specs=[vmem] * 3,
        out_shape=[shape] * 3,
        compiler_params=params,
    )(new_gain, summed, *others)


def solution(mesh):
    placed = (
        P("band", "pair", None, None, None),
        P("band", "pair", None, None, None, None),
        P("pair", None),
        P("pair"),
        P("band", None, None, "pair"),
        P("band", None, None, "pair"),
        P("band", None, None, "pair"),
    )
    return jax.shard_map(
        local,
        mesh=mesh,
        in_specs=placed,
        out_specs=(
            P("band", None, None, "pair"),
            P("band", None, None, "pair"),
            P("band", None, None, "pair"),
        ),
        check_vma=False,
    )
```

```python
import math

import jax
import jax.numpy as jnp
import numpy as np
from jax import lax
from jax.experimental import pallas as pl
from jax.experimental.pallas import tpu as pltpu
from jax.sharding import PartitionSpec as P


P_SIZE = 8
TILE = 32
LANES = 128
HALF = LANES // 2
GROUP = LANES // TILE
PIECES = 2

ridge = 0.05
penalty = 0.25


def fit_matrix(freq_count, term_count):
    positions = (np.arange(freq_count) + 0.5) / freq_count
    basis = np.stack(
        [
            math.comb(term_count - 1, degree)
            * positions**degree
            * (1.0 - positions) ** (term_count - 1 - degree)
            for degree in range(term_count)
        ],
        axis=1,
    )
    normal = basis.T @ basis + ridge * np.eye(term_count)
    factor = np.linalg.cholesky(normal)
    half = np.linalg.solve(factor, basis.T)
    return half.T @ half


class Plan:
    def __init__(self, directions, stations, pairs, blocks, times, cells):
        self.k = directions
        self.sl = stations
        self.zn = pairs // 2
        self.blocks = blocks
        self.times = times
        self.steps = cells // LANES
        self.total = blocks * self.steps
        self.per = stations // TILE
        self.parts = 1 if self.per else TILE // stations
        self.rows = 2 * directions + 8 * ((blocks + 7) // 8)
        assert 2 * stations <= LANES and directions == 32 and times <= 8 and self.steps == 8

    def lane(self, rows=None):
        return lax.broadcasted_iota(jnp.int32, (self.k if rows is None else rows, LANES), 1)

    def owner(self, me, device):
        return (device % 2) == (me % 2), (device // 2) ^ (me // 2)

    def record(self, me, own_ref, sib_ref, device, row):
        same, slot = self.owner(me, device)
        own = own_ref[slot, row : row + self.k, :]
        sib = sib_ref[slot, row : row + self.k, :]
        return jnp.where(same, own, sib)

    def fetch(self, me, own_ref, sib_ref, tile, row):
        lane = self.lane()
        part, spot = lane // HALF, lane % TILE
        if self.sl == HALF:
            device = lax.shift_right_logical(tile, 1)
            sub = lax.bitwise_and(tile, 1)
            rec = self.record(me, own_ref, sib_ref, device, row)
            return jnp.where(sub == 1, pltpu.roll(rec, LANES - TILE, 1), rec)
        if self.per:
            device = tile // self.per
            sub = tile - device * self.per
            rec = self.record(me, own_ref, sib_ref, device, row)
            return take(rec, part * self.sl + sub * TILE + spot)
        value = None
        for r in range(self.parts):
            rec = self.record(me, own_ref, sib_ref, tile * self.parts + r, row)
            here = take(rec, part * self.sl + spot % self.sl)
            value = here if value is None else jnp.where(spot // self.sl == r, here, value)
        return value

    def place(self, terms, side, sub):
        lane = self.lane()
        if self.sl == HALF:
            moved = pltpu.roll(terms, TILE if side == 0 else LANES - TILE, 1)
            return jnp.where(lane // TILE % 2 == sub, jnp.where(sub == side, terms, moved), 0.0)
        part, spot = lane // self.sl % 2, lane % self.sl
        start = part * HALF + side * TILE
        if self.per:
            value = take(terms, start + spot % TILE)
            keep = spot // TILE == sub
        else:
            value = take(terms, start + sub * self.sl + spot)
            keep = lane < 2 * self.sl
        return jnp.where(keep, value, 0.0)

    def spread(self, me, tile, terms, side, own_ref, sib_ref):
        if self.per:
            device = tile // self.per
            spots = [(device, tile - device * self.per)]
        else:
            spots = [(tile * self.parts + r, r) for r in range(self.parts)]
        for device, sub in spots:
            value = self.place(terms, side, sub)
            same, slot = self.owner(me, device)
            own_ref[slot] = own_ref[slot] + jnp.where(same, value, 0.0)
            sib_ref[slot] = sib_ref[slot] + jnp.where(same, 0.0, value)

    def record_of(self, raw_ref):
        pieces = [raw_ref[0, 0], raw_ref[0, 1]]
        if 2 * self.sl < LANES:
            pieces.append(jnp.zeros((self.k, LANES - 2 * self.sl), jnp.float32))
        return jnp.concatenate(pieces, axis=1)


def take(value, lanes):
    return jnp.take_along_axis(value, lanes, axis=1, mode="promise_in_bounds")


def pieces(value, count):
    result = []
    for _ in range(count):
        result.append(value.astype(jnp.bfloat16))
        value = value - result[-1].astype(jnp.float32)
    return result


def matmul(lhs, rhs):
    return jnp.dot(lhs, rhs, preferred_element_type=jnp.float32)


def eights(value):
    return [value[8 * i : 8 * i + 8] for i in range(value.shape[0] // 8)]


def pack_kernel(plan, tiles_hbm, counts_hbm, gains_hbm, targets_hbm, mult_hbm, out_ref, meta_ref, mrec_ref, *scratch):
    bufs, sems = scratch[:-1], scratch[-1]
    copies = [
        pltpu.make_async_copy(src, dst, sems.at[i])
        for i, (src, dst) in enumerate(zip((gains_hbm, targets_hbm, mult_hbm, tiles_hbm, counts_hbm), bufs))
    ]
    for copy in copies:
        copy.start()
    for copy in copies:
        copy.wait()
    gains_ref, targets_ref, mult_ref, tiles_ref, counts_ref = bufs
    k = plan.k
    gain = plan.record_of(gains_ref)
    target = plan.record_of(targets_ref)
    mult = plan.record_of(mult_ref)
    out_ref[:k] = gain
    out_ref[k : 2 * k] = gain - penalty * (gain - target + mult)
    mrec_ref[...] = mult
    lane = plan.lane(8)
    sub = lax.broadcasted_iota(jnp.int32, (8, LANES), 0)
    meta = jnp.zeros((8, LANES), jnp.int32)
    for base in range(0, plan.blocks, 8):
        rows = jnp.zeros((8, LANES), jnp.int32)
        for n in range(base, min(base + 8, plan.blocks)):
            ids = jnp.where(lane // TILE % 2 == 0, tiles_ref[n, 0], tiles_ref[n, 1])
            rows = jnp.where(sub == n - base, ids, rows)
            for j, number in enumerate((tiles_ref[n, 0], tiles_ref[n, 1], counts_ref[n])):
                meta = jnp.where(lane == 3 * n + j, number, meta)
        out_ref[2 * k + base : 2 * k + base + 8] = rows.astype(jnp.float32)
    meta_ref[...] = meta


def load_kernel(plan, vis_hbm, coh_hbm, vis_ref, coh_ref, vis_buf, coh_buf, sems):
    chunks = 4
    per = plan.steps // chunks
    copies = []
    for n in range(plan.blocks):
        for c in range(chunks):
            lanes = pl.ds(c * per * LANES, per * LANES)
            copies.append(
                pltpu.make_async_copy(
                    coh_hbm.at[0, n, :, :, :, lanes],
                    coh_buf.at[n, :, :, :, lanes],
                    sems.at[n * chunks + c],
                )
            )
    last = pltpu.make_async_copy(vis_hbm.at[0], vis_buf, sems.at[plan.blocks * chunks])
    for copy in copies:
        copy.start()
    last.start()
    for n in range(plan.blocks):
        for c in range(chunks):
            copies[n * chunks + c].wait()

            def convert(t, carry, n=n, c=c):
                for index in range(c * per, (c + 1) * per):
                    lanes = pl.ds(index * LANES, LANES)
                    real = coh_buf[n, t, 0, :, lanes].astype(jnp.float32)
                    imag = coh_buf[n, t, 1, :, lanes].astype(jnp.float32)
                    q = n * plan.steps + index
                    coh_ref[q, t, 0] = real
                    coh_ref[q, t, 1] = real + imag
                    coh_ref[q, t, 2] = real - imag
                return carry

            lax.fori_loop(0, plan.times, convert, 0)
    last.wait()
    for n in range(plan.blocks):
        for part in range(2):
            value = vis_buf[n, :, part, :]
            for index in range(plan.steps):
                vis_ref[n * plan.steps + index, part] = value[:, index * LANES : (index + 1) * LANES]


def table_kernel(plan, spread_ref, narrow_ref, fold_ref):
    record = lax.broadcasted_iota(jnp.int32, (LANES, LANES), 0)
    cell = lax.broadcasted_iota(jnp.int32, (LANES, LANES), 1)
    spread = cell // TILE - record
    narrow = record // TILE - cell
    fold = TILE + record % TILE - cell
    for part in range(2):
        for index in range(plan.steps):
            span = slice((2 * index + part) * LANES, (2 * index + part + 1) * LANES)
            offset = -(part * HALF + index * GROUP)
            spread_ref[:, span] = jnp.where(spread == offset, 1.0, 0.0).astype(jnp.bfloat16)
            narrow_ref[span, :] = jnp.where(narrow == offset, 1.0, 0.0).astype(jnp.bfloat16)
        hit = jnp.where(fold == -part * HALF, 1.0, 0.0).astype(jnp.bfloat16)
        fold_ref[part * LANES : (part + 1) * LANES, :] = hit


def block_gradients(
    plan, meta_ref, tile_gains, vis_ref, coh_ref, spread_ref, narrow_ref, fold_ref,
    right_ref, wide_ref, second_ref, first_ref, model_ref, error_ref,
):
    k, times, steps = plan.k, plan.times, plan.steps
    shift = steps.bit_length() - 1
    lane_k = plan.lane()
    lane = plan.lane(8)
    sample = lax.broadcasted_iota(jnp.int32, (8, LANES), 0)
    lefts = [piece for left, _ in tile_gains for piece in pieces(left, 3)]
    lefts = matmul(jnp.concatenate(lefts, axis=0), spread_ref[...])
    for n in range(plan.blocks):
        rows = [lefts[(3 * n + i) * k : (3 * n + i + 1) * k] for i in range(3)]
        value = rows[0] + rows[1] + rows[2]
        for index in range(steps):
            for part in range(2):
                start = (2 * index + part) * LANES
                wide_ref[n * steps + index, part] = value[:, start : start + LANES]
    for n, (left, right) in enumerate(tile_gains):
        pairs = jnp.where(lane_k // TILE % 2 == 0, right, pltpu.roll(right, TILE, 1))
        other = pltpu.roll(pairs, HALF, 1)
        right_ref[n, 0] = jnp.where(lane_k < HALF, pairs, other)
        right_ref[n, 1] = jnp.where(lane_k < HALF, other, pairs)
        second_ref[n] = jnp.zeros((2, k, LANES), jnp.float32)

    def where_is(q):
        q = jnp.int32(q)
        return lax.shift_right_logical(q, shift), lax.bitwise_and(q, steps - 1)

    def residual(q):
        n, index = where_is(q)
        lr, li = wide_ref[q, 0], wide_ref[q, 1]
        rr, ri = right_ref[n, 0], right_ref[n, 1]
        pr = lr * rr + li * ri
        pi = li * rr - lr * ri
        ps = pr + pi
        for t in range(times):
            both = sum(eights(ps * coh_ref[q, t, 0]))
            model_ref[0, 8 * t : 8 * t + 8] = both - sum(eights(pi * coh_ref[q, t, 1]))
            model_ref[1, 8 * t : 8 * t + 8] = both - sum(eights(pr * coh_ref[q, t, 2]))
        mr, mi = (sum(model_ref[part, pl.ds(j, times, stride=8), :] for j in range(8)) for part in range(2))
        upper = index * GROUP + lane // TILE - lane % TILE
        differ = meta_ref[0, 3 * n] != meta_ref[0, 3 * n + 1]
        bound = jnp.where(differ, steps * LANES, 0)
        keep = ((upper < bound) & (sample < meta_ref[0, 3 * n + 2]))[:times]
        er = jnp.where(keep, vis_ref[q, 0] - mr, 0.0)
        ei = jnp.where(keep, vis_ref[q, 1] - mi, 0.0)
        slot = lax.bitwise_and(jnp.int32(q), 1)
        error_ref[slot, 0, :times] = er + ei
        error_ref[slot, 1, :times] = ei
        error_ref[slot, 2, :times] = er

    def gradient(q):
        n, index = where_is(q)
        slot = lax.bitwise_and(jnp.int32(q), 1)
        sums = [None] * 3
        for t in range(times):
            for j, c in enumerate((0, 2, 1)):
                e = error_ref[slot, j, pl.ds(t, 8, stride=0), :]
                value = [e * part for part in eights(coh_ref[q, t, c])]
                sums[j] = value if t == 0 else [x + y for x, y in zip(sums[j], value)]
        both, lone_re, lone_im = (jnp.concatenate(value, axis=0) for value in sums)
        acc_re = both - lone_re
        acc_im = both - lone_im
        lr, li = wide_ref[q, 0], wide_ref[q, 1]
        rr, ri = right_ref[n, 0], right_ref[n, 1]
        second_ref[n, 0] = second_ref[n, 0] + (acc_re * lr + acc_im * li)
        second_ref[n, 1] = second_ref[n, 1] + (acc_re * li - acc_im * lr)
        terms = jnp.concatenate([acc_re * rr - acc_im * ri, acc_re * ri + acc_im * rr], axis=1)
        lanes = pl.ds(pl.multiple_of(index * 2 * LANES, 2 * LANES), 2 * LANES)
        for i, piece in enumerate(pieces(terms, PIECES)):
            rows = pl.ds(pl.multiple_of((n * PIECES + i) * k, k), k)
            first_ref[rows, lanes] = piece

    final = plan.total - 1

    def step(q, carry):
        gradient(q)
        residual(q + 1)
        return carry

    residual(0)
    lax.fori_loop(0, final, step, 0)
    gradient(final)

    parts = []
    for n in range(plan.blocks):
        parts += pieces(jnp.concatenate([second_ref[n, 0], second_ref[n, 1]], axis=1), PIECES)
    value = matmul(jnp.concatenate(parts, axis=0), fold_ref[...])
    value = value + matmul(first_ref[...], narrow_ref[...])
    return [
        sum(value[(n * PIECES + i) * k : (n * PIECES + i + 1) * k] for i in range(PIECES))
        for n in range(plan.blocks)
    ]


def first_kernel(plan, meta_ref, own_ref, sib_ref, vis_ref, coh_ref, spread_ref, narrow_ref, fold_ref, out_ref, *scratch):
    fixed = (vis_ref, coh_ref, spread_ref, narrow_ref, fold_ref)
    me = lax.axis_index("pair")
    tile_gains = [
        [plan.fetch(me, own_ref, sib_ref, meta_ref[0, 3 * n + side], 0) for side in range(2)]
        for n in range(plan.blocks)
    ]
    for n, terms in enumerate(block_gradients(plan, meta_ref, tile_gains, *fixed, *scratch)):
        out_ref[n] = terms


def second_kernel(
    plan, step_size, meta_ref, own_ref, sib_ref, term_own_ref, term_sib_ref, mult_ref,
    vis_ref, coh_ref, spread_ref, narrow_ref, fold_ref, part_own_ref, part_sib_ref, rest_ref, *scratch,
):
    fixed = (vis_ref, coh_ref, spread_ref, narrow_ref, fold_ref)
    k = plan.k
    me = lax.axis_index("pair")
    wanted = [meta_ref[0, 3 * n + side] for n in range(plan.blocks) for side in range(2)]
    if plan.per:
        wanted += [me * plan.per + s for s in range(plan.per)]
    else:
        wanted += [me // plan.parts]
    labels = [t.astype(jnp.float32) for t in wanted]

    def gather(slot, sums):
        for pay_ref, term_ref in ((own_ref, term_own_ref), (sib_ref, term_sib_ref)):
            ids_all = pay_ref[slot, 2 * k : plan.rows, :]
            for n in range(plan.blocks):
                ids = ids_all[n : n + 1]
                terms = term_ref[slot, n]
                sums = [s + jnp.where(ids == label, terms, 0.0) for s, label in zip(sums, labels)]
        return sums

    sums = [jnp.zeros((k, LANES), jnp.float32) for _ in wanted]
    if plan.zn <= 4:
        for slot in range(plan.zn):
            sums = gather(slot, sums)
    else:
        sums = lax.fori_loop(0, plan.zn, gather, sums)
    sums = [s + pltpu.roll(s, LANES - TILE, 1) for s in sums]

    tile_gains = [
        [
            plan.fetch(me, own_ref, sib_ref, wanted[2 * n + side], k) + step_size * sums[2 * n + side]
            for side in range(2)
        ]
        for n in range(plan.blocks)
    ]

    mine = sums[2 * plan.blocks :]
    if plan.per:
        own_sum = sum(plan.place(value, 0, s) for s, value in enumerate(mine))
    else:
        own_sum = plan.place(mine[0], 0, me % plan.parts)
    start = own_ref[0, :k, :]
    base = own_ref[0, k : 2 * k, :]
    pull = base - (1.0 - penalty) * start
    rest = (1.0 - penalty) * (base + step_size * own_sum) + pull
    rest_ref[0] = rest
    rest_ref[1] = rest + mult_ref[...]

    part_own_ref[...] = jnp.zeros_like(part_own_ref)
    part_sib_ref[...] = jnp.zeros_like(part_sib_ref)
    for n, terms in enumerate(block_gradients(plan, meta_ref, tile_gains, *fixed, *scratch)):
        for side in range(2):
            plan.spread(me, meta_ref[0, 3 * n + side], terms, side, part_own_ref, part_sib_ref)


def fit_kernel(plan, fit, gain_ref, own_ref, *refs):
    others, (gain_out, target_out, mult_out) = refs[:-3], refs[-3:]
    sl = plan.sl
    band = lax.axis_index("band")
    total = None
    for m, ref in enumerate((own_ref,) + tuple(others)):
        factor = jnp.float32(0.0)
        for f in range(fit.shape[0]):
            factor = jnp.where(band == f, jnp.float32(fit[f, f ^ m]), factor)
        value = factor * ref[...]
        total = value if total is None else total + value
    change = own_ref[...] - total
    gain = gain_ref[...]
    for part in range(2):
        lanes = slice(part * sl, (part + 1) * sl)
        gain_out[0, part] = gain[:, lanes]
        target_out[0, part] = total[:, lanes]
        mult_out[0, part] = change[:, lanes]


def exchange(value, axis, size, mask):
    return lax.ppermute(value, axis, [(i, i ^ mask) for i in range(size)])


def local(visibilities, coherencies, block_tiles, sample_counts, gains, targets, multipliers):
    pairs = lax.axis_size("pair")
    bands = lax.axis_size("band")
    _, blocks, times, _, directions, cells = coherencies.shape
    stations = gains.shape[3]
    plan = Plan(directions, stations, pairs, blocks, times, cells)
    k, zn = plan.k, plan.zn
    tile_count = stations * pairs // TILE
    step_size = 0.25 * tile_count * k / (times * TILE * blocks * pairs)

    smem = pl.BlockSpec(memory_space=pltpu.SMEM)
    vmem = pl.BlockSpec(memory_space=pltpu.VMEM)
    hbm = pl.BlockSpec(memory_space=pltpu.HBM)
    stay = lambda value: pltpu.with_memory_space_constraint(value, pltpu.HBM)
    f32 = lambda *shape: jax.ShapeDtypeStruct(shape, jnp.float32)
    scratch = [
        pltpu.VMEM((blocks, 2, k, LANES), jnp.float32),
        pltpu.VMEM((plan.total, 2, k, LANES), jnp.float32),
        pltpu.VMEM((blocks, 2, k, LANES), jnp.float32),
        pltpu.VMEM((blocks * PIECES * k, 2 * cells), jnp.bfloat16),
        pltpu.VMEM((2, 8 * times, LANES), jnp.float32),
        pltpu.VMEM((2, 3, 8, LANES), jnp.float32),
    ]
    params = pltpu.CompilerParams(vmem_limit_bytes=16 << 20)

    payload, meta, mult_rec = pl.pallas_call(
        lambda *refs: pack_kernel(plan, *refs),
        name="pack",
        in_specs=[hbm] * 5,
        out_specs=[vmem] * 3,
        out_shape=[f32(plan.rows, LANES), jax.ShapeDtypeStruct((8, LANES), jnp.int32), f32(k, LANES)],
        scratch_shapes=[pltpu.VMEM(gains.shape, jnp.float32)] * 3
        + [
            pltpu.SMEM(block_tiles.shape, jnp.int32),
            pltpu.SMEM(sample_counts.shape, jnp.int32),
            pltpu.SemaphoreType.DMA((5,)),
        ],
        compiler_params=params,
    )(*map(stay, (block_tiles, sample_counts, gains, targets, multipliers)))

    vis, coh = pl.pallas_call(
        lambda *refs: load_kernel(plan, *refs),
        name="load",
        in_specs=[hbm] * 2,
        out_specs=[vmem] * 2,
        out_shape=[f32(plan.total, 2, times, LANES), f32(plan.total, times, 3, k, LANES)],
        scratch_shapes=[
            pltpu.VMEM((blocks, times, 2, cells), jnp.float32),
            pltpu.VMEM((blocks, times, 2, k, cells), jnp.bfloat16),
            pltpu.SemaphoreType.DMA((4 * blocks + 1,)),
        ],
        compiler_params=params,
    )(stay(visibilities), stay(coherencies))

    bf16 = lambda *shape: jax.ShapeDtypeStruct(shape, jnp.bfloat16)
    tables = pl.pallas_call(
        lambda *refs: table_kernel(plan, *refs),
        name="tables",
        in_specs=[],
        out_specs=[vmem] * 3,
        out_shape=[
            bf16(LANES, 2 * cells),
            bf16(2 * cells, LANES),
            bf16(2 * LANES, LANES),
        ],
        compiler_params=params,
    )()

    def gather(value):
        parts = [value] + [exchange(value, "pair", pairs, 2 * m) for m in range(1, zn)]
        own = jnp.stack(parts)
        return own, exchange(own, "pair", pairs, 1)

    own, sib = gather(payload)

    terms = pl.pallas_call(
        lambda *refs: first_kernel(plan, *refs),
        name="first",
        in_specs=[smem] + [vmem] * 7,
        out_specs=vmem,
        out_shape=f32(blocks, k, LANES),
        scratch_shapes=scratch,
        compiler_params=params,
    )(meta, own, sib, vis, coh, *tables)

    term_own, term_sib = gather(terms)
    part_own, part_sib, rest = pl.pallas_call(
        lambda *refs: second_kernel(plan, step_size, *refs),
        name="second",
        in_specs=[smem] + [vmem] * 10,
        out_specs=[vmem, vmem, vmem],
        out_shape=[f32(zn, k, LANES), f32(zn, k, LANES), f32(2, k, LANES)],
        scratch_shapes=scratch,
        compiler_params=params,
    )(meta, own, sib, term_own, term_sib, mult_rec, vis, coh, *tables)

    crossed = exchange(part_sib, "pair", pairs, 1)
    total = part_own[0] + crossed[0]
    for m in range(1, zn):
        total = total + exchange(part_own[m] + crossed[m], "pair", pairs, 2 * m)
    new_gain = rest[0] + step_size * total
    summed = rest[1] + step_size * total

    others = [exchange(summed, "band", bands, m) for m in range(1, bands)]
    shape = f32(*gains.shape)
    return pl.pallas_call(
        lambda *refs: fit_kernel(plan, fit_matrix(bands, P_SIZE), *refs),
        name="fit",
        in_specs=[vmem] * (2 + len(others)),
        out_specs=[vmem] * 3,
        out_shape=[shape] * 3,
        compiler_params=params,
    )(new_gain, summed, *others)


def solution(mesh):
    placed = (
        P("band", "pair", None, None, None),
        P("band", "pair", None, None, None, None),
        P("pair", None),
        P("pair"),
        P("band", None, None, "pair"),
        P("band", None, None, "pair"),
        P("band", None, None, "pair"),
    )
    return jax.shard_map(
        local,
        mesh=mesh,
        in_specs=placed,
        out_specs=(
            P("band", None, None, "pair"),
            P("band", None, None, "pair"),
            P("band", None, None, "pair"),
        ),
        check_vma=False,
    )
```

```python
import math

import jax
import jax.numpy as jnp
import numpy as np
from jax import lax
from jax.experimental import pallas as pl
from jax.experimental.pallas import tpu as pltpu
from jax.sharding import PartitionSpec as P


P_SIZE = 8
TILE = 32
LANES = 128
HALF = LANES // 2
GROUP = LANES // TILE
PIECES = 2

ridge = 0.05
penalty = 0.25


def fit_matrix(freq_count, term_count):
    positions = (np.arange(freq_count) + 0.5) / freq_count
    basis = np.stack(
        [
            math.comb(term_count - 1, degree)
            * positions**degree
            * (1.0 - positions) ** (term_count - 1 - degree)
            for degree in range(term_count)
        ],
        axis=1,
    )
    normal = basis.T @ basis + ridge * np.eye(term_count)
    factor = np.linalg.cholesky(normal)
    half = np.linalg.solve(factor, basis.T)
    return half.T @ half


class Plan:
    def __init__(self, directions, stations, pairs, blocks, times, cells):
        self.k = directions
        self.sl = stations
        self.zn = pairs // 2
        self.blocks = blocks
        self.times = times
        self.cells = cells
        self.steps = cells // LANES
        self.total = blocks * self.steps
        self.per = stations // TILE
        self.parts = 1 if self.per else TILE // stations
        self.rows = 2 * directions + 8 * ((blocks + 7) // 8)
        assert 2 * stations <= LANES and directions == 32 and times <= 8 and self.steps == 8

    def lane(self, rows=None):
        return lax.broadcasted_iota(jnp.int32, (self.k if rows is None else rows, LANES), 1)

    def owner(self, me, device):
        return (device % 2) == (me % 2), (device // 2) ^ (me // 2)

    def record(self, me, own_ref, sib_ref, device, row):
        same, slot = self.owner(me, device)
        own = own_ref[slot, row : row + self.k, :]
        sib = sib_ref[slot, row : row + self.k, :]
        return jnp.where(same, own, sib)

    def fetch(self, me, own_ref, sib_ref, tile, row):
        lane = self.lane()
        part, spot = lane // HALF, lane % TILE
        if self.sl == HALF:
            device = lax.shift_right_logical(tile, 1)
            sub = lax.bitwise_and(tile, 1)
            rec = self.record(me, own_ref, sib_ref, device, row)
            return jnp.where(sub == 1, pltpu.roll(rec, LANES - TILE, 1), rec)
        if self.per:
            device = tile // self.per
            sub = tile - device * self.per
            rec = self.record(me, own_ref, sib_ref, device, row)
            return take(rec, part * self.sl + sub * TILE + spot)
        value = None
        for r in range(self.parts):
            rec = self.record(me, own_ref, sib_ref, tile * self.parts + r, row)
            here = take(rec, part * self.sl + spot % self.sl)
            value = here if value is None else jnp.where(spot // self.sl == r, here, value)
        return value

    def place(self, terms, side, sub):
        lane = self.lane()
        if self.sl == HALF:
            moved = pltpu.roll(terms, TILE if side == 0 else LANES - TILE, 1)
            return jnp.where(lane // TILE % 2 == sub, jnp.where(sub == side, terms, moved), 0.0)
        part, spot = lane // self.sl % 2, lane % self.sl
        start = part * HALF + side * TILE
        if self.per:
            value = take(terms, start + spot % TILE)
            keep = spot // TILE == sub
        else:
            value = take(terms, start + sub * self.sl + spot)
            keep = lane < 2 * self.sl
        return jnp.where(keep, value, 0.0)

    def spread(self, me, tile, terms, side, own_ref, sib_ref):
        if self.per:
            device = tile // self.per
            spots = [(device, tile - device * self.per)]
        else:
            spots = [(tile * self.parts + r, r) for r in range(self.parts)]
        for device, sub in spots:
            value = self.place(terms, side, sub)
            same, slot = self.owner(me, device)
            own_ref[slot] = own_ref[slot] + jnp.where(same, value, 0.0)
            sib_ref[slot] = sib_ref[slot] + jnp.where(same, 0.0, value)

    def record_of(self, raw_ref):
        pieces = [raw_ref[0, 0], raw_ref[0, 1]]
        if 2 * self.sl < LANES:
            pieces.append(jnp.zeros((self.k, LANES - 2 * self.sl), jnp.float32))
        return jnp.concatenate(pieces, axis=1)


def take(value, lanes):
    return jnp.take_along_axis(value, lanes, axis=1, mode="promise_in_bounds")


def pieces(value, count):
    result = []
    for _ in range(count):
        result.append(value.astype(jnp.bfloat16))
        value = value - result[-1].astype(jnp.float32)
    return result


def matmul(lhs, rhs):
    return jnp.dot(lhs, rhs, preferred_element_type=jnp.float32)


def eights(value):
    return [value[8 * i : 8 * i + 8] for i in range(value.shape[0] // 8)]


def pack_kernel(plan, tiles_hbm, counts_hbm, gains_hbm, targets_hbm, mult_hbm, out_ref, meta_ref, bound_ref, mrec_ref, *scratch):
    bufs, sems = scratch[:-1], scratch[-1]
    copies = [
        pltpu.make_async_copy(src, dst, sems.at[i])
        for i, (src, dst) in enumerate(zip((gains_hbm, targets_hbm, mult_hbm, tiles_hbm, counts_hbm), bufs))
    ]
    for copy in copies:
        copy.start()
    for copy in copies:
        copy.wait()
    gains_ref, targets_ref, mult_ref, tiles_ref, counts_ref = bufs
    k = plan.k
    gain = plan.record_of(gains_ref)
    target = plan.record_of(targets_ref)
    mult = plan.record_of(mult_ref)
    out_ref[:k] = gain
    out_ref[k : 2 * k] = gain - penalty * (gain - target + mult)
    mrec_ref[...] = mult
    lane = plan.lane(8)
    sub = lax.broadcasted_iota(jnp.int32, (8, LANES), 0)
    tiles = tiles_ref[...]
    counts = counts_ref[...]
    meta = jnp.zeros((8, LANES), jnp.int32)
    for base in range(0, plan.blocks, 8):
        rows = jnp.zeros((8, LANES), jnp.int32)
        for n in range(base, min(base + 8, plan.blocks)):
            one, two, count = tiles[n, 0], tiles[n, 1], counts[0, n]
            ids = jnp.where(lane // TILE % 2 == 0, one, two)
            rows = jnp.where(sub == n - base, ids, rows)
            meta = jnp.where(lane == 2 * n, one, jnp.where(lane == 2 * n + 1, two, meta))
            bound_ref[n, 0] = jnp.full((8, LANES), count, jnp.int32)
            bound_ref[n, 1] = jnp.full((8, LANES), jnp.where(one != two, plan.cells, 0), jnp.int32)
        out_ref[2 * k + base : 2 * k + base + 8] = rows.astype(jnp.float32)
    meta_ref[...] = meta


def load_kernel(plan, vis_hbm, coh_hbm, vis_ref, coh_ref, vis_buf, coh_buf, sems):
    chunks = 4
    per = plan.steps // chunks
    copies = []
    for n in range(plan.blocks):
        for c in range(chunks):
            lanes = pl.ds(c * per * LANES, per * LANES)
            copies.append(
                pltpu.make_async_copy(
                    coh_hbm.at[0, n, :, :, :, lanes],
                    coh_buf.at[n, :, :, :, lanes],
                    sems.at[n * chunks + c],
                )
            )
    last = pltpu.make_async_copy(vis_hbm.at[0], vis_buf, sems.at[plan.blocks * chunks])
    for copy in copies:
        copy.start()
    last.start()
    for n in range(plan.blocks):
        for c in range(chunks):
            copies[n * chunks + c].wait()

            def convert(t, carry, n=n, c=c):
                for index in range(c * per, (c + 1) * per):
                    lanes = pl.ds(index * LANES, LANES)
                    real = coh_buf[n, t, 0, :, lanes].astype(jnp.float32)
                    imag = coh_buf[n, t, 1, :, lanes].astype(jnp.float32)
                    q = n * plan.steps + index
                    coh_ref[q, t, 0] = real
                    coh_ref[q, t, 1] = real + imag
                    coh_ref[q, t, 2] = real - imag
                return carry

            lax.fori_loop(0, plan.times, convert, 0)
    last.wait()
    for n in range(plan.blocks):
        for part in range(2):
            value = vis_buf[n, :, part, :]
            for index in range(plan.steps):
                vis_ref[n * plan.steps + index, part] = value[:, index * LANES : (index + 1) * LANES]


def table_kernel(plan, spread_ref, narrow_ref, fold_ref):
    record = lax.broadcasted_iota(jnp.int32, (LANES, LANES), 0)
    cell = lax.broadcasted_iota(jnp.int32, (LANES, LANES), 1)
    spread = cell // TILE - record
    narrow = record // TILE - cell
    fold = TILE + record % TILE - cell
    for part in range(2):
        for index in range(plan.steps):
            span = slice((2 * index + part) * LANES, (2 * index + part + 1) * LANES)
            offset = -(part * HALF + index * GROUP)
            spread_ref[:, span] = jnp.where(spread == offset, 1.0, 0.0).astype(jnp.bfloat16)
            narrow_ref[span, :] = jnp.where(narrow == offset, 1.0, 0.0).astype(jnp.bfloat16)
        hit = jnp.where(fold == -part * HALF, 1.0, 0.0).astype(jnp.bfloat16)
        fold_ref[part * LANES : (part + 1) * LANES, :] = hit


def block_gradients(
    plan, bound_ref, tile_gains, vis_ref, coh_ref, spread_ref, narrow_ref, fold_ref,
    right_ref, wide_ref, second_ref, first_ref, model_ref, error_ref,
):
    k, times, steps = plan.k, plan.times, plan.steps
    shift = steps.bit_length() - 1
    lane_k = plan.lane()
    lane = plan.lane(8)
    sample = lax.broadcasted_iota(jnp.int32, (8, LANES), 0)
    lefts = [piece for left, _ in tile_gains for piece in pieces(left, 3)]
    lefts = matmul(jnp.concatenate(lefts, axis=0), spread_ref[...])
    for n in range(plan.blocks):
        rows = [lefts[(3 * n + i) * k : (3 * n + i + 1) * k] for i in range(3)]
        value = rows[0] + rows[1] + rows[2]
        for index in range(steps):
            for part in range(2):
                start = (2 * index + part) * LANES
                wide_ref[n * steps + index, part] = value[:, start : start + LANES]
    for n, (left, right) in enumerate(tile_gains):
        pairs = jnp.where(lane_k // TILE % 2 == 0, right, pltpu.roll(right, TILE, 1))
        other = pltpu.roll(pairs, HALF, 1)
        right_ref[n, 0] = jnp.where(lane_k < HALF, pairs, other)
        right_ref[n, 1] = jnp.where(lane_k < HALF, other, pairs)
        second_ref[n] = jnp.zeros((2, k, LANES), jnp.float32)

    def where_is(q):
        q = jnp.int32(q)
        return lax.shift_right_logical(q, shift), lax.bitwise_and(q, steps - 1)

    def residual(q):
        n, index = where_is(q)
        lr, li = wide_ref[q, 0], wide_ref[q, 1]
        rr, ri = right_ref[n, 0], right_ref[n, 1]
        pr = lr * rr + li * ri
        pi = li * rr - lr * ri
        ps = pr + pi
        for t in range(times):
            both = sum(eights(ps * coh_ref[q, t, 0]))
            model_ref[0, 8 * t : 8 * t + 8] = both - sum(eights(pi * coh_ref[q, t, 1]))
            model_ref[1, 8 * t : 8 * t + 8] = both - sum(eights(pr * coh_ref[q, t, 2]))
        mr, mi = (sum(model_ref[part, pl.ds(j, times, stride=8), :] for j in range(8)) for part in range(2))
        upper = index * GROUP + lane // TILE - lane % TILE
        keep = ((upper < bound_ref[n, 1]) & (sample < bound_ref[n, 0]))[:times]
        er = jnp.where(keep, vis_ref[q, 0] - mr, 0.0)
        ei = jnp.where(keep, vis_ref[q, 1] - mi, 0.0)
        slot = lax.bitwise_and(jnp.int32(q), 1)
        error_ref[slot, 0, :times] = er + ei
        error_ref[slot, 1, :times] = ei
        error_ref[slot, 2, :times] = er

    def gradient(q):
        n, index = where_is(q)
        slot = lax.bitwise_and(jnp.int32(q), 1)
        sums = [None] * 3
        for t in range(times):
            for j, c in enumerate((0, 2, 1)):
                e = error_ref[slot, j, pl.ds(t, 8, stride=0), :]
                value = [e * part for part in eights(coh_ref[q, t, c])]
                sums[j] = value if t == 0 else [x + y for x, y in zip(sums[j], value)]
        both, lone_re, lone_im = (jnp.concatenate(value, axis=0) for value in sums)
        acc_re = both - lone_re
        acc_im = both - lone_im
        lr, li = wide_ref[q, 0], wide_ref[q, 1]
        rr, ri = right_ref[n, 0], right_ref[n, 1]
        second_ref[n, 0] = second_ref[n, 0] + (acc_re * lr + acc_im * li)
        second_ref[n, 1] = second_ref[n, 1] + (acc_re * li - acc_im * lr)
        terms = jnp.concatenate([acc_re * rr - acc_im * ri, acc_re * ri + acc_im * rr], axis=1)
        lanes = pl.ds(pl.multiple_of(index * 2 * LANES, 2 * LANES), 2 * LANES)
        for i, piece in enumerate(pieces(terms, PIECES)):
            rows = pl.ds(pl.multiple_of((n * PIECES + i) * k, k), k)
            first_ref[rows, lanes] = piece

    final = plan.total - 1

    def step(q, carry):
        gradient(q)
        residual(q + 1)
        return carry

    residual(0)
    lax.fori_loop(0, final, step, 0, unroll=5)
    gradient(final)

    parts = []
    for n in range(plan.blocks):
        parts += pieces(jnp.concatenate([second_ref[n, 0], second_ref[n, 1]], axis=1), PIECES)
    value = matmul(jnp.concatenate(parts, axis=0), fold_ref[...])
    value = value + matmul(first_ref[...], narrow_ref[...])
    return [
        sum(value[(n * PIECES + i) * k : (n * PIECES + i + 1) * k] for i in range(PIECES))
        for n in range(plan.blocks)
    ]


def tile_ids(plan, meta_ref):
    meta = meta_ref[0:1, :]
    return [meta[0, i] for i in range(2 * plan.blocks)]


def first_kernel(plan, meta_ref, bound_ref, own_ref, sib_ref, vis_ref, coh_ref, spread_ref, narrow_ref, fold_ref, out_ref, *scratch):
    fixed = (vis_ref, coh_ref, spread_ref, narrow_ref, fold_ref)
    me = lax.axis_index("pair")
    records = [plan.fetch(me, own_ref, sib_ref, tile, 0) for tile in tile_ids(plan, meta_ref)]
    tile_gains = [records[2 * n : 2 * n + 2] for n in range(plan.blocks)]
    for n, terms in enumerate(block_gradients(plan, bound_ref, tile_gains, *fixed, *scratch)):
        out_ref[n] = terms


def gather_terms(plan, pay_ref, term_ref, tiles):
    k = plan.k
    labels = [tile.astype(jnp.float32) for tile in tiles]

    def add(slot, sums):
        ids_all = pay_ref[slot, 2 * k : plan.rows, :]
        for n in range(plan.blocks):
            ids = ids_all[n : n + 1]
            terms = term_ref[slot, n]
            sums = [s + jnp.where(ids == label, terms, 0.0) for s, label in zip(sums, labels)]
        return sums

    sums = [jnp.zeros((k, LANES), jnp.float32) for _ in labels]
    if plan.zn <= 4:
        for slot in range(plan.zn):
            sums = add(slot, sums)
    else:
        sums = lax.fori_loop(0, plan.zn, add, sums)
    return [s + pltpu.roll(s, LANES - TILE, 1) for s in sums]


def own_tiles(plan, me):
    if plan.per:
        return [me * plan.per + s for s in range(plan.per)]
    return [me // plan.parts]


def near_kernel(plan, step_size, meta_ref, own_ref, sib_ref, term_ref, records_ref, mine_ref):
    me = lax.axis_index("pair")
    tiles = tile_ids(plan, meta_ref)
    for i, value in enumerate(gather_terms(plan, own_ref, term_ref, tiles)):
        records_ref[i] = plan.fetch(me, own_ref, sib_ref, tiles[i], plan.k) + step_size * value
    for i, value in enumerate(gather_terms(plan, own_ref, term_ref, own_tiles(plan, me))):
        mine_ref[i] = value


def rest_kernel(plan, step_size, own_ref, sib_ref, term_ref, mine_ref, mult_ref, rest_ref):
    k = plan.k
    me = lax.axis_index("pair")
    sums = gather_terms(plan, sib_ref, term_ref, own_tiles(plan, me))
    mine = [mine_ref[i] + value for i, value in enumerate(sums)]
    if plan.per:
        own_sum = sum(plan.place(value, 0, s) for s, value in enumerate(mine))
    else:
        own_sum = plan.place(mine[0], 0, me % plan.parts)
    start = own_ref[0, :k, :]
    base = own_ref[0, k : 2 * k, :]
    pull = base - (1.0 - penalty) * start
    rest = (1.0 - penalty) * (base + step_size * own_sum) + pull
    rest_ref[0] = rest
    rest_ref[1] = rest + mult_ref[...]


def second_kernel(
    plan, step_size, meta_ref, bound_ref, sib_ref, term_ref, records_ref,
    vis_ref, coh_ref, spread_ref, narrow_ref, fold_ref, part_own_ref, part_sib_ref, *scratch,
):
    fixed = (vis_ref, coh_ref, spread_ref, narrow_ref, fold_ref)
    me = lax.axis_index("pair")
    tiles = tile_ids(plan, meta_ref)
    sums = gather_terms(plan, sib_ref, term_ref, tiles)
    records = [records_ref[i] + step_size * value for i, value in enumerate(sums)]
    tile_gains = [records[2 * n : 2 * n + 2] for n in range(plan.blocks)]
    part_own_ref[...] = jnp.zeros_like(part_own_ref)
    part_sib_ref[...] = jnp.zeros_like(part_sib_ref)
    for n, terms in enumerate(block_gradients(plan, bound_ref, tile_gains, *fixed, *scratch)):
        for side in range(2):
            plan.spread(me, tiles[2 * n + side], terms, side, part_own_ref, part_sib_ref)


def fit_kernel(plan, fit, gain_ref, own_ref, *refs):
    others, (gain_out, target_out, mult_out) = refs[:-3], refs[-3:]
    sl = plan.sl
    band = lax.axis_index("band")
    total = None
    for m, ref in enumerate((own_ref,) + tuple(others)):
        factor = jnp.float32(0.0)
        for f in range(fit.shape[0]):
            factor = jnp.where(band == f, jnp.float32(fit[f, f ^ m]), factor)
        value = factor * ref[...]
        total = value if total is None else total + value
    change = own_ref[...] - total
    gain = gain_ref[...]
    for part in range(2):
        lanes = slice(part * sl, (part + 1) * sl)
        gain_out[0, part] = gain[:, lanes]
        target_out[0, part] = total[:, lanes]
        mult_out[0, part] = change[:, lanes]


def exchange(value, axis, size, mask):
    return lax.ppermute(value, axis, [(i, i ^ mask) for i in range(size)])


def local(visibilities, coherencies, block_tiles, sample_counts, gains, targets, multipliers):
    pairs = lax.axis_size("pair")
    bands = lax.axis_size("band")
    _, blocks, times, _, directions, cells = coherencies.shape
    stations = gains.shape[3]
    plan = Plan(directions, stations, pairs, blocks, times, cells)
    k, zn = plan.k, plan.zn
    tile_count = stations * pairs // TILE
    step_size = 0.25 * tile_count * k / (times * TILE * blocks * pairs)

    vmem = pl.BlockSpec(memory_space=pltpu.VMEM)
    hbm = pl.BlockSpec(memory_space=pltpu.HBM)
    stay = lambda value: pltpu.with_memory_space_constraint(value, pltpu.HBM)
    i32 = lambda *shape: jax.ShapeDtypeStruct(shape, jnp.int32)
    f32 = lambda *shape: jax.ShapeDtypeStruct(shape, jnp.float32)
    scratch = [
        pltpu.VMEM((blocks, 2, k, LANES), jnp.float32),
        pltpu.VMEM((plan.total, 2, k, LANES), jnp.float32),
        pltpu.VMEM((blocks, 2, k, LANES), jnp.float32),
        pltpu.VMEM((blocks * PIECES * k, 2 * cells), jnp.bfloat16),
        pltpu.VMEM((2, 8 * times, LANES), jnp.float32),
        pltpu.VMEM((2, 3, 8, LANES), jnp.float32),
    ]
    params = pltpu.CompilerParams(vmem_limit_bytes=16 << 20)

    payload, meta, bounds, mult_rec = pl.pallas_call(
        lambda *refs: pack_kernel(plan, *refs),
        name="pack",
        in_specs=[hbm] * 5,
        out_specs=[vmem] * 4,
        out_shape=[f32(plan.rows, LANES), i32(8, LANES), i32(blocks, 2, 8, LANES), f32(k, LANES)],
        scratch_shapes=[pltpu.VMEM(gains.shape, jnp.float32)] * 3
        + [
            pltpu.VMEM(block_tiles.shape, jnp.int32),
            pltpu.VMEM((1, blocks), jnp.int32),
            pltpu.SemaphoreType.DMA((5,)),
        ],
        compiler_params=params,
    )(*map(stay, (block_tiles, sample_counts.reshape(1, blocks), gains, targets, multipliers)))

    vis, coh = pl.pallas_call(
        lambda *refs: load_kernel(plan, *refs),
        name="load",
        in_specs=[hbm] * 2,
        out_specs=[vmem] * 2,
        out_shape=[f32(plan.total, 2, times, LANES), f32(plan.total, times, 3, k, LANES)],
        scratch_shapes=[
            pltpu.VMEM((blocks, times, 2, cells), jnp.float32),
            pltpu.VMEM((blocks, times, 2, k, cells), jnp.bfloat16),
            pltpu.SemaphoreType.DMA((4 * blocks + 1,)),
        ],
        compiler_params=params,
    )(stay(visibilities), stay(coherencies))

    bf16 = lambda *shape: jax.ShapeDtypeStruct(shape, jnp.bfloat16)
    tables = pl.pallas_call(
        lambda *refs: table_kernel(plan, *refs),
        name="tables",
        in_specs=[],
        out_specs=[vmem] * 3,
        out_shape=[
            bf16(LANES, 2 * cells),
            bf16(2 * cells, LANES),
            bf16(2 * LANES, LANES),
        ],
        compiler_params=params,
    )()

    def gather(value):
        parts = [value] + [exchange(value, "pair", pairs, 2 * m) for m in range(1, zn)]
        own = jnp.stack(parts)
        return own, exchange(own, "pair", pairs, 1)

    own, sib = gather(payload)

    terms = pl.pallas_call(
        lambda *refs: first_kernel(plan, *refs),
        name="first",
        in_specs=[vmem] * 9,
        out_specs=vmem,
        out_shape=f32(blocks, k, LANES),
        scratch_shapes=scratch,
        compiler_params=params,
    )(meta, bounds, own, sib, vis, coh, *tables)

    term_own, term_sib = gather(terms)
    records, mine = pl.pallas_call(
        lambda *refs: near_kernel(plan, step_size, *refs),
        name="near",
        in_specs=[vmem] * 4,
        out_specs=[vmem] * 2,
        out_shape=[f32(2 * blocks, k, LANES), f32(max(plan.per, 1), k, LANES)],
        compiler_params=params,
    )(meta, own, sib, term_own)
    part_own, part_sib = pl.pallas_call(
        lambda *refs: second_kernel(plan, step_size, *refs),
        name="second",
        in_specs=[vmem] * 10,
        out_specs=[vmem] * 2,
        out_shape=[f32(zn, k, LANES)] * 2,
        scratch_shapes=scratch,
        compiler_params=params,
    )(meta, bounds, sib, term_sib, records, vis, coh, *tables)

    rest = pl.pallas_call(
        lambda *refs: rest_kernel(plan, step_size, *refs),
        name="rest",
        in_specs=[vmem] * 5,
        out_specs=vmem,
        out_shape=f32(2, k, LANES),
        compiler_params=params,
    )(own, sib, term_sib, mine, mult_rec)
    crossed = exchange(part_sib, "pair", pairs, 1)
    total = part_own[0] + crossed[0]
    for m in range(1, zn):
        total = total + exchange(part_own[m] + crossed[m], "pair", pairs, 2 * m)
    new_gain = rest[0] + step_size * total
    summed = rest[1] + step_size * total

    others = [exchange(summed, "band", bands, m) for m in range(1, bands)]
    shape = f32(*gains.shape)
    return pl.pallas_call(
        lambda *refs: fit_kernel(plan, fit_matrix(bands, P_SIZE), *refs),
        name="fit",
        in_specs=[vmem] * (2 + len(others)),
        out_specs=[vmem] * 3,
        out_shape=[shape] * 3,
        compiler_params=params,
    )(new_gain, summed, *others)


def solution(mesh):
    placed = (
        P("band", "pair", None, None, None),
        P("band", "pair", None, None, None, None),
        P("pair", None),
        P("pair"),
        P("band", None, None, "pair"),
        P("band", None, None, "pair"),
        P("band", None, None, "pair"),
    )
    return jax.shard_map(
        local,
        mesh=mesh,
        in_specs=placed,
        out_specs=(
            P("band", None, None, "pair"),
            P("band", None, None, "pair"),
            P("band", None, None, "pair"),
        ),
        check_vma=False,
    )
```

```python
import math

import jax
import jax.numpy as jnp
import numpy as np
from jax import lax
from jax.experimental import pallas as pl
from jax.experimental.pallas import tpu as pltpu
from jax.sharding import PartitionSpec as P


P_SIZE = 8
TILE = 32
LANES = 128
HALF = LANES // 2
GROUP = LANES // TILE
PIECES = 2

ridge = 0.05
penalty = 0.25


def fit_matrix(freq_count, term_count):
    positions = (np.arange(freq_count) + 0.5) / freq_count
    basis = np.stack(
        [
            math.comb(term_count - 1, degree)
            * positions**degree
            * (1.0 - positions) ** (term_count - 1 - degree)
            for degree in range(term_count)
        ],
        axis=1,
    )
    normal = basis.T @ basis + ridge * np.eye(term_count)
    factor = np.linalg.cholesky(normal)
    half = np.linalg.solve(factor, basis.T)
    return half.T @ half


class Plan:
    def __init__(self, directions, stations, pairs, blocks, times, cells):
        self.k = directions
        self.sl = stations
        self.zn = pairs // 2
        self.blocks = blocks
        self.times = times
        self.cells = cells
        self.steps = cells // LANES
        self.total = blocks * self.steps
        self.per = stations // TILE
        self.parts = 1 if self.per else TILE // stations
        self.rows = 2 * directions + 8 * ((blocks + 7) // 8)
        assert 2 * stations <= LANES and directions == 32 and times <= 8 and self.steps == 8

    def lane(self, rows=None):
        return lax.broadcasted_iota(jnp.int32, (self.k if rows is None else rows, LANES), 1)

    def owner(self, me, device):
        slot = lax.shift_right_logical(device ^ me, 1)
        crossed = lax.bitwise_and(device ^ me, 1)
        return crossed == jnp.where(slot == 0, 0, 1), slot

    def record(self, me, own_ref, sib_ref, device, row):
        same, slot = self.owner(me, device)
        own = own_ref[slot, row : row + self.k, :]
        sib = sib_ref[slot, row : row + self.k, :]
        return jnp.where(same, own, sib)

    def fetch(self, me, own_ref, sib_ref, tile, row):
        lane = self.lane()
        part, spot = lane // HALF, lane % TILE
        if self.sl == HALF:
            device = lax.shift_right_logical(tile, 1)
            sub = lax.bitwise_and(tile, 1)
            rec = self.record(me, own_ref, sib_ref, device, row)
            return jnp.where(sub == 1, pltpu.roll(rec, LANES - TILE, 1), rec)
        if self.per:
            device = tile // self.per
            sub = tile - device * self.per
            rec = self.record(me, own_ref, sib_ref, device, row)
            return take(rec, part * self.sl + sub * TILE + spot)
        value = None
        for r in range(self.parts):
            rec = self.record(me, own_ref, sib_ref, tile * self.parts + r, row)
            here = take(rec, part * self.sl + spot % self.sl)
            value = here if value is None else jnp.where(spot // self.sl == r, here, value)
        return value

    def place(self, terms, side, sub):
        lane = self.lane()
        if self.sl == HALF:
            moved = pltpu.roll(terms, TILE if side == 0 else LANES - TILE, 1)
            return jnp.where(lane // TILE % 2 == sub, jnp.where(sub == side, terms, moved), 0.0)
        part, spot = lane // self.sl % 2, lane % self.sl
        start = part * HALF + side * TILE
        if self.per:
            value = take(terms, start + spot % TILE)
            keep = spot // TILE == sub
        else:
            value = take(terms, start + sub * self.sl + spot)
            keep = lane < 2 * self.sl
        return jnp.where(keep, value, 0.0)

    def spread(self, me, tile, terms, side, own_ref, sib_ref):
        if self.per:
            device = tile // self.per
            spots = [(device, tile - device * self.per)]
        else:
            spots = [(tile * self.parts + r, r) for r in range(self.parts)]
        for device, sub in spots:
            value = self.place(terms, side, sub)
            same, slot = self.owner(me, device)
            own_ref[slot] = own_ref[slot] + jnp.where(same, value, 0.0)
            sib_ref[slot] = sib_ref[slot] + jnp.where(same, 0.0, value)

    def record_of(self, raw_ref):
        pieces = [raw_ref[0, 0], raw_ref[0, 1]]
        if 2 * self.sl < LANES:
            pieces.append(jnp.zeros((self.k, LANES - 2 * self.sl), jnp.float32))
        return jnp.concatenate(pieces, axis=1)


def take(value, lanes):
    return jnp.take_along_axis(value, lanes, axis=1, mode="promise_in_bounds")


def pieces(value, count):
    result = []
    for _ in range(count):
        result.append(value.astype(jnp.bfloat16))
        value = value - result[-1].astype(jnp.float32)
    return result


def matmul(lhs, rhs):
    return jnp.dot(lhs, rhs, preferred_element_type=jnp.float32)


def eights(value):
    return [value[8 * i : 8 * i + 8] for i in range(value.shape[0] // 8)]


def pack_kernel(plan, tiles_hbm, counts_hbm, gains_hbm, targets_hbm, mult_hbm, out_ref, meta_ref, bound_ref, mrec_ref, *scratch):
    bufs, sems = scratch[:-1], scratch[-1]
    copies = [
        pltpu.make_async_copy(src, dst, sems.at[i])
        for i, (src, dst) in enumerate(zip((gains_hbm, targets_hbm, mult_hbm, tiles_hbm, counts_hbm), bufs))
    ]
    for copy in copies:
        copy.start()
    for copy in copies:
        copy.wait()
    gains_ref, targets_ref, mult_ref, tiles_ref, counts_ref = bufs
    k = plan.k
    gain = plan.record_of(gains_ref)
    target = plan.record_of(targets_ref)
    mult = plan.record_of(mult_ref)
    out_ref[:k] = gain
    out_ref[k : 2 * k] = gain - penalty * (gain - target + mult)
    mrec_ref[...] = mult
    lane = plan.lane(8)
    sub = lax.broadcasted_iota(jnp.int32, (8, LANES), 0)
    tiles = tiles_ref[...]
    counts = counts_ref[...]
    meta = jnp.zeros((8, LANES), jnp.int32)
    for base in range(0, plan.blocks, 8):
        rows = jnp.zeros((8, LANES), jnp.int32)
        for n in range(base, min(base + 8, plan.blocks)):
            one, two, count = tiles[n, 0], tiles[n, 1], counts[0, n]
            ids = jnp.where(lane // TILE % 2 == 0, one, two)
            rows = jnp.where(sub == n - base, ids, rows)
            meta = jnp.where(lane == 2 * n, one, jnp.where(lane == 2 * n + 1, two, meta))
            bound_ref[n, 0] = jnp.full((8, LANES), count, jnp.int32)
            bound_ref[n, 1] = jnp.full((8, LANES), jnp.where(one != two, plan.cells, 0), jnp.int32)
        out_ref[2 * k + base : 2 * k + base + 8] = rows.astype(jnp.float32)
    meta_ref[...] = meta


def load_kernel(plan, vis_hbm, coh_hbm, vis_ref, coh_ref, vis_buf, coh_buf, sems):
    chunks = 4
    per = plan.steps // chunks
    copies = []
    for n in range(plan.blocks):
        for c in range(chunks):
            lanes = pl.ds(c * per * LANES, per * LANES)
            copies.append(
                pltpu.make_async_copy(
                    coh_hbm.at[0, n, :, :, :, lanes],
                    coh_buf.at[n, :, :, :, lanes],
                    sems.at[n * chunks + c],
                )
            )
    last = pltpu.make_async_copy(vis_hbm.at[0], vis_buf, sems.at[plan.blocks * chunks])
    for copy in copies:
        copy.start()
    last.start()
    for n in range(plan.blocks):
        for c in range(chunks):
            copies[n * chunks + c].wait()

            def convert(t, carry, n=n, c=c):
                for index in range(c * per, (c + 1) * per):
                    lanes = pl.ds(index * LANES, LANES)
                    real = coh_buf[n, t, 0, :, lanes].astype(jnp.float32)
                    imag = coh_buf[n, t, 1, :, lanes].astype(jnp.float32)
                    q = n * plan.steps + index
                    coh_ref[q, t, 0] = real
                    coh_ref[q, t, 1] = real + imag
                    coh_ref[q, t, 2] = real - imag
                return carry

            lax.fori_loop(0, plan.times, convert, 0)
    last.wait()
    for n in range(plan.blocks):
        for part in range(2):
            value = vis_buf[n, :, part, :]
            for index in range(plan.steps):
                vis_ref[n * plan.steps + index, part] = value[:, index * LANES : (index + 1) * LANES]


def table_kernel(plan, spread_ref, narrow_ref, fold_ref):
    record = lax.broadcasted_iota(jnp.int32, (LANES, LANES), 0)
    cell = lax.broadcasted_iota(jnp.int32, (LANES, LANES), 1)
    spread = cell // TILE - record
    narrow = record // TILE - cell
    fold = TILE + record % TILE - cell
    for part in range(2):
        for index in range(plan.steps):
            span = slice((2 * index + part) * LANES, (2 * index + part + 1) * LANES)
            offset = -(part * HALF + index * GROUP)
            spread_ref[:, span] = jnp.where(spread == offset, 1.0, 0.0).astype(jnp.bfloat16)
            narrow_ref[span, :] = jnp.where(narrow == offset, 1.0, 0.0).astype(jnp.bfloat16)
        hit = jnp.where(fold == -part * HALF, 1.0, 0.0).astype(jnp.bfloat16)
        fold_ref[part * LANES : (part + 1) * LANES, :] = hit


def block_gradients(
    plan, bound_ref, tile_gains, vis_ref, coh_ref, spread_ref, narrow_ref, fold_ref,
    right_ref, wide_ref, second_ref, first_ref, model_ref, error_ref,
):
    k, times, steps = plan.k, plan.times, plan.steps
    shift = steps.bit_length() - 1
    lane_k = plan.lane()
    lane = plan.lane(8)
    sample = lax.broadcasted_iota(jnp.int32, (8, LANES), 0)
    lefts = [piece for left, _ in tile_gains for piece in pieces(left, 3)]
    lefts = matmul(jnp.concatenate(lefts, axis=0), spread_ref[...])
    for n in range(plan.blocks):
        rows = [lefts[(3 * n + i) * k : (3 * n + i + 1) * k] for i in range(3)]
        value = rows[0] + rows[1] + rows[2]
        for index in range(steps):
            for part in range(2):
                start = (2 * index + part) * LANES
                wide_ref[n * steps + index, part] = value[:, start : start + LANES]
    for n, (left, right) in enumerate(tile_gains):
        pairs = jnp.where(lane_k // TILE % 2 == 0, right, pltpu.roll(right, TILE, 1))
        other = pltpu.roll(pairs, HALF, 1)
        right_ref[n, 0] = jnp.where(lane_k < HALF, pairs, other)
        right_ref[n, 1] = jnp.where(lane_k < HALF, other, pairs)
        second_ref[n] = jnp.zeros((2, k, LANES), jnp.float32)

    def where_is(q):
        q = jnp.int32(q)
        return lax.shift_right_logical(q, shift), lax.bitwise_and(q, steps - 1)

    def residual(q):
        n, index = where_is(q)
        lr, li = wide_ref[q, 0], wide_ref[q, 1]
        rr, ri = right_ref[n, 0], right_ref[n, 1]
        pr = lr * rr + li * ri
        pi = li * rr - lr * ri
        ps = pr + pi
        for t in range(times):
            both = sum(eights(ps * coh_ref[q, t, 0]))
            model_ref[0, 8 * t : 8 * t + 8] = both - sum(eights(pi * coh_ref[q, t, 1]))
            model_ref[1, 8 * t : 8 * t + 8] = both - sum(eights(pr * coh_ref[q, t, 2]))
        mr, mi = (sum(model_ref[part, pl.ds(j, times, stride=8), :] for j in range(8)) for part in range(2))
        upper = index * GROUP + lane // TILE - lane % TILE
        keep = ((upper < bound_ref[n, 1]) & (sample < bound_ref[n, 0]))[:times]
        er = jnp.where(keep, vis_ref[q, 0] - mr, 0.0)
        ei = jnp.where(keep, vis_ref[q, 1] - mi, 0.0)
        slot = lax.bitwise_and(jnp.int32(q), 1)
        error_ref[slot, 0, :times] = er + ei
        error_ref[slot, 1, :times] = ei
        error_ref[slot, 2, :times] = er

    def gradient(q):
        n, index = where_is(q)
        slot = lax.bitwise_and(jnp.int32(q), 1)
        sums = [None] * 3
        for t in range(times):
            for j, c in enumerate((0, 2, 1)):
                e = error_ref[slot, j, pl.ds(t, 8, stride=0), :]
                value = [e * part for part in eights(coh_ref[q, t, c])]
                sums[j] = value if t == 0 else [x + y for x, y in zip(sums[j], value)]
        both, lone_re, lone_im = (jnp.concatenate(value, axis=0) for value in sums)
        acc_re = both - lone_re
        acc_im = both - lone_im
        lr, li = wide_ref[q, 0], wide_ref[q, 1]
        rr, ri = right_ref[n, 0], right_ref[n, 1]
        second_ref[n, 0] = second_ref[n, 0] + (acc_re * lr + acc_im * li)
        second_ref[n, 1] = second_ref[n, 1] + (acc_re * li - acc_im * lr)
        terms = jnp.concatenate([acc_re * rr - acc_im * ri, acc_re * ri + acc_im * rr], axis=1)
        lanes = pl.ds(pl.multiple_of(index * 2 * LANES, 2 * LANES), 2 * LANES)
        for i, piece in enumerate(pieces(terms, PIECES)):
            rows = pl.ds(pl.multiple_of((n * PIECES + i) * k, k), k)
            first_ref[rows, lanes] = piece

    final = plan.total - 1

    def step(q, carry):
        gradient(q)
        residual(q + 1)
        return carry

    residual(0)
    lax.fori_loop(0, final, step, 0, unroll=5)
    gradient(final)

    parts = []
    for n in range(plan.blocks):
        parts += pieces(jnp.concatenate([second_ref[n, 0], second_ref[n, 1]], axis=1), PIECES)
    value = matmul(jnp.concatenate(parts, axis=0), fold_ref[...])
    value = value + matmul(first_ref[...], narrow_ref[...])
    return [
        sum(value[(n * PIECES + i) * k : (n * PIECES + i + 1) * k] for i in range(PIECES))
        for n in range(plan.blocks)
    ]


def tile_ids(plan, meta_ref):
    meta = meta_ref[0:1, :]
    return [meta[0, i] for i in range(2 * plan.blocks)]


def first_kernel(plan, meta_ref, bound_ref, own_ref, sib_ref, vis_ref, coh_ref, spread_ref, narrow_ref, fold_ref, out_ref, *scratch):
    fixed = (vis_ref, coh_ref, spread_ref, narrow_ref, fold_ref)
    me = lax.axis_index("pair")
    records = [plan.fetch(me, own_ref, sib_ref, tile, 0) for tile in tile_ids(plan, meta_ref)]
    tile_gains = [records[2 * n : 2 * n + 2] for n in range(plan.blocks)]
    for n, terms in enumerate(block_gradients(plan, bound_ref, tile_gains, *fixed, *scratch)):
        out_ref[n] = terms


def gather_terms(plan, pay_ref, term_ref, tiles):
    k = plan.k
    labels = [tile.astype(jnp.float32) for tile in tiles]

    def add(slot, sums):
        ids_all = pay_ref[slot, 2 * k : plan.rows, :]
        for n in range(plan.blocks):
            ids = ids_all[n : n + 1]
            terms = term_ref[slot, n]
            sums = [s + jnp.where(ids == label, terms, 0.0) for s, label in zip(sums, labels)]
        return sums

    sums = [jnp.zeros((k, LANES), jnp.float32) for _ in labels]
    if plan.zn <= 4:
        for slot in range(plan.zn):
            sums = add(slot, sums)
    else:
        sums = lax.fori_loop(0, plan.zn, add, sums)
    return [s + pltpu.roll(s, LANES - TILE, 1) for s in sums]


def own_tiles(plan, me):
    if plan.per:
        return [me * plan.per + s for s in range(plan.per)]
    return [me // plan.parts]


def near_kernel(plan, step_size, meta_ref, own_ref, sib_ref, term_ref, records_ref, mine_ref):
    me = lax.axis_index("pair")
    tiles = tile_ids(plan, meta_ref)
    for i, value in enumerate(gather_terms(plan, own_ref, term_ref, tiles)):
        records_ref[i] = plan.fetch(me, own_ref, sib_ref, tiles[i], plan.k) + step_size * value
    for i, value in enumerate(gather_terms(plan, own_ref, term_ref, own_tiles(plan, me))):
        mine_ref[i] = value


def rest_kernel(plan, step_size, own_ref, sib_ref, term_ref, mine_ref, mult_ref, rest_ref):
    k = plan.k
    me = lax.axis_index("pair")
    sums = gather_terms(plan, sib_ref, term_ref, own_tiles(plan, me))
    mine = [mine_ref[i] + value for i, value in enumerate(sums)]
    if plan.per:
        own_sum = sum(plan.place(value, 0, s) for s, value in enumerate(mine))
    else:
        own_sum = plan.place(mine[0], 0, me % plan.parts)
    start = own_ref[0, :k, :]
    base = own_ref[0, k : 2 * k, :]
    pull = base - (1.0 - penalty) * start
    rest = (1.0 - penalty) * (base + step_size * own_sum) + pull
    rest_ref[0] = rest
    rest_ref[1] = rest + mult_ref[...]


def second_kernel(
    plan, step_size, meta_ref, bound_ref, sib_ref, term_ref, records_ref,
    vis_ref, coh_ref, spread_ref, narrow_ref, fold_ref, part_own_ref, part_sib_ref, *scratch,
):
    fixed = (vis_ref, coh_ref, spread_ref, narrow_ref, fold_ref)
    me = lax.axis_index("pair")
    tiles = tile_ids(plan, meta_ref)
    sums = gather_terms(plan, sib_ref, term_ref, tiles)
    records = [records_ref[i] + step_size * value for i, value in enumerate(sums)]
    tile_gains = [records[2 * n : 2 * n + 2] for n in range(plan.blocks)]
    part_own_ref[...] = jnp.zeros_like(part_own_ref)
    part_sib_ref[...] = jnp.zeros_like(part_sib_ref)
    for n, terms in enumerate(block_gradients(plan, bound_ref, tile_gains, *fixed, *scratch)):
        for side in range(2):
            plan.spread(me, tiles[2 * n + side], terms, side, part_own_ref, part_sib_ref)


def fit_kernel(plan, fit, gain_ref, own_ref, *refs):
    others, (gain_out, target_out, mult_out) = refs[:-3], refs[-3:]
    sl = plan.sl
    band = lax.axis_index("band")
    total = None
    for m, ref in enumerate((own_ref,) + tuple(others)):
        factor = jnp.float32(0.0)
        for f in range(fit.shape[0]):
            factor = jnp.where(band == f, jnp.float32(fit[f, f ^ m]), factor)
        value = factor * ref[...]
        total = value if total is None else total + value
    change = own_ref[...] - total
    gain = gain_ref[...]
    for part in range(2):
        lanes = slice(part * sl, (part + 1) * sl)
        gain_out[0, part] = gain[:, lanes]
        target_out[0, part] = total[:, lanes]
        mult_out[0, part] = change[:, lanes]


def exchange(value, axis, size, mask):
    return lax.ppermute(value, axis, [(i, i ^ mask) for i in range(size)])


def local(visibilities, coherencies, block_tiles, sample_counts, gains, targets, multipliers):
    pairs = lax.axis_size("pair")
    bands = lax.axis_size("band")
    _, blocks, times, _, directions, cells = coherencies.shape
    stations = gains.shape[3]
    plan = Plan(directions, stations, pairs, blocks, times, cells)
    k, zn = plan.k, plan.zn
    tile_count = stations * pairs // TILE
    step_size = 0.25 * tile_count * k / (times * TILE * blocks * pairs)

    vmem = pl.BlockSpec(memory_space=pltpu.VMEM)
    hbm = pl.BlockSpec(memory_space=pltpu.HBM)
    stay = lambda value: pltpu.with_memory_space_constraint(value, pltpu.HBM)
    i32 = lambda *shape: jax.ShapeDtypeStruct(shape, jnp.int32)
    f32 = lambda *shape: jax.ShapeDtypeStruct(shape, jnp.float32)
    scratch = [
        pltpu.VMEM((blocks, 2, k, LANES), jnp.float32),
        pltpu.VMEM((plan.total, 2, k, LANES), jnp.float32),
        pltpu.VMEM((blocks, 2, k, LANES), jnp.float32),
        pltpu.VMEM((blocks * PIECES * k, 2 * cells), jnp.bfloat16),
        pltpu.VMEM((2, 8 * times, LANES), jnp.float32),
        pltpu.VMEM((2, 3, 8, LANES), jnp.float32),
    ]
    params = pltpu.CompilerParams(vmem_limit_bytes=16 << 20)

    payload, meta, bounds, mult_rec = pl.pallas_call(
        lambda *refs: pack_kernel(plan, *refs),
        name="pack",
        in_specs=[hbm] * 5,
        out_specs=[vmem] * 4,
        out_shape=[f32(plan.rows, LANES), i32(8, LANES), i32(blocks, 2, 8, LANES), f32(k, LANES)],
        scratch_shapes=[pltpu.VMEM(gains.shape, jnp.float32)] * 3
        + [
            pltpu.VMEM(block_tiles.shape, jnp.int32),
            pltpu.VMEM((1, blocks), jnp.int32),
            pltpu.SemaphoreType.DMA((5,)),
        ],
        compiler_params=params,
    )(*map(stay, (block_tiles, sample_counts.reshape(1, blocks), gains, targets, multipliers)))

    vis, coh = pl.pallas_call(
        lambda *refs: load_kernel(plan, *refs),
        name="load",
        in_specs=[hbm] * 2,
        out_specs=[vmem] * 2,
        out_shape=[f32(plan.total, 2, times, LANES), f32(plan.total, times, 3, k, LANES)],
        scratch_shapes=[
            pltpu.VMEM((blocks, times, 2, cells), jnp.float32),
            pltpu.VMEM((blocks, times, 2, k, cells), jnp.bfloat16),
            pltpu.SemaphoreType.DMA((4 * blocks + 1,)),
        ],
        compiler_params=params,
    )(stay(visibilities), stay(coherencies))

    bf16 = lambda *shape: jax.ShapeDtypeStruct(shape, jnp.bfloat16)
    tables = pl.pallas_call(
        lambda *refs: table_kernel(plan, *refs),
        name="tables",
        in_specs=[],
        out_specs=[vmem] * 3,
        out_shape=[
            bf16(LANES, 2 * cells),
            bf16(2 * cells, LANES),
            bf16(2 * LANES, LANES),
        ],
        compiler_params=params,
    )()

    def gather(value):
        parts = [value] + [exchange(value, "pair", pairs, 2 * m + 1) for m in range(1, zn)]
        own = jnp.stack(parts)
        return own, exchange(own, "pair", pairs, 1)

    own, sib = gather(payload)

    terms = pl.pallas_call(
        lambda *refs: first_kernel(plan, *refs),
        name="first",
        in_specs=[vmem] * 9,
        out_specs=vmem,
        out_shape=f32(blocks, k, LANES),
        scratch_shapes=scratch,
        compiler_params=params,
    )(meta, bounds, own, sib, vis, coh, *tables)

    term_own, term_sib = gather(terms)
    records, mine = pl.pallas_call(
        lambda *refs: near_kernel(plan, step_size, *refs),
        name="near",
        in_specs=[vmem] * 4,
        out_specs=[vmem] * 2,
        out_shape=[f32(2 * blocks, k, LANES), f32(max(plan.per, 1), k, LANES)],
        compiler_params=params,
    )(meta, own, sib, term_own)
    part_own, part_sib = pl.pallas_call(
        lambda *refs: second_kernel(plan, step_size, *refs),
        name="second",
        in_specs=[vmem] * 10,
        out_specs=[vmem] * 2,
        out_shape=[f32(zn, k, LANES)] * 2,
        scratch_shapes=scratch,
        compiler_params=params,
    )(meta, bounds, sib, term_sib, records, vis, coh, *tables)

    rest = pl.pallas_call(
        lambda *refs: rest_kernel(plan, step_size, *refs),
        name="rest",
        in_specs=[vmem] * 5,
        out_specs=vmem,
        out_shape=f32(2, k, LANES),
        compiler_params=params,
    )(own, sib, term_sib, mine, mult_rec)
    crossed = exchange(part_sib, "pair", pairs, 1)
    total = part_own[0] + crossed[0]
    for m in range(1, zn):
        total = total + exchange(part_own[m] + crossed[m], "pair", pairs, 2 * m + 1)
    new_gain = rest[0] + step_size * total
    summed = rest[1] + step_size * total

    others = [exchange(summed, "band", bands, m) for m in range(1, bands)]
    shape = f32(*gains.shape)
    return pl.pallas_call(
        lambda *refs: fit_kernel(plan, fit_matrix(bands, P_SIZE), *refs),
        name="fit",
        in_specs=[vmem] * (2 + len(others)),
        out_specs=[vmem] * 3,
        out_shape=[shape] * 3,
        compiler_params=params,
    )(new_gain, summed, *others)


def solution(mesh):
    placed = (
        P("band", "pair", None, None, None),
        P("band", "pair", None, None, None, None),
        P("pair", None),
        P("pair"),
        P("band", None, None, "pair"),
        P("band", None, None, "pair"),
        P("band", None, None, "pair"),
    )
    return jax.shard_map(
        local,
        mesh=mesh,
        in_specs=placed,
        out_specs=(
            P("band", None, None, "pair"),
            P("band", None, None, "pair"),
            P("band", None, None, "pair"),
        ),
        check_vma=False,
    )
```

```python
import math

import jax
import jax.numpy as jnp
import numpy as np
from jax import lax
from jax.experimental import pallas as pl
from jax.experimental.pallas import tpu as pltpu
from jax.sharding import PartitionSpec as P


P_SIZE = 8
TILE = 32
LANES = 128
HALF = LANES // 2
GROUP = LANES // TILE
PIECES = 2

ridge = 0.05
penalty = 0.25


def fit_matrix(freq_count, term_count):
    positions = (np.arange(freq_count) + 0.5) / freq_count
    basis = np.stack(
        [
            math.comb(term_count - 1, degree)
            * positions**degree
            * (1.0 - positions) ** (term_count - 1 - degree)
            for degree in range(term_count)
        ],
        axis=1,
    )
    normal = basis.T @ basis + ridge * np.eye(term_count)
    factor = np.linalg.cholesky(normal)
    half = np.linalg.solve(factor, basis.T)
    return half.T @ half


class Plan:
    def __init__(self, directions, stations, pairs, blocks, times, cells):
        self.k = directions
        self.sl = stations
        self.zn = pairs // 2
        self.blocks = blocks
        self.times = times
        self.cells = cells
        self.steps = cells // LANES
        self.total = blocks * self.steps
        self.per = stations // TILE
        self.parts = 1 if self.per else TILE // stations
        self.rows = 2 * directions + 8 * ((blocks + 7) // 8)
        assert 2 * stations <= LANES and directions == 32 and times <= 8 and self.steps == 8

    def lane(self, rows=None):
        return lax.broadcasted_iota(jnp.int32, (self.k if rows is None else rows, LANES), 1)

    def owner(self, me, device):
        slot = lax.shift_right_logical(device ^ me, 1)
        crossed = lax.bitwise_and(device ^ me, 1)
        return crossed == jnp.where(slot == 0, 0, 1), slot

    def record(self, me, own_ref, sib_ref, device, row):
        same, slot = self.owner(me, device)
        own = own_ref[slot, row : row + self.k, :]
        sib = sib_ref[slot, row : row + self.k, :]
        return jnp.where(same, own, sib)

    def fetch(self, me, own_ref, sib_ref, tile, row):
        lane = self.lane()
        part, spot = lane // HALF, lane % TILE
        if self.sl == HALF:
            device = lax.shift_right_logical(tile, 1)
            sub = lax.bitwise_and(tile, 1)
            rec = self.record(me, own_ref, sib_ref, device, row)
            return jnp.where(sub == 1, pltpu.roll(rec, LANES - TILE, 1), rec)
        if self.per:
            device = tile // self.per
            sub = tile - device * self.per
            rec = self.record(me, own_ref, sib_ref, device, row)
            return take(rec, part * self.sl + sub * TILE + spot)
        value = None
        for r in range(self.parts):
            rec = self.record(me, own_ref, sib_ref, tile * self.parts + r, row)
            here = take(rec, part * self.sl + spot % self.sl)
            value = here if value is None else jnp.where(spot // self.sl == r, here, value)
        return value

    def place(self, terms, side, sub):
        lane = self.lane()
        if self.sl == HALF:
            moved = pltpu.roll(terms, TILE if side == 0 else LANES - TILE, 1)
            return jnp.where(lane // TILE % 2 == sub, jnp.where(sub == side, terms, moved), 0.0)
        part, spot = lane // self.sl % 2, lane % self.sl
        start = part * HALF + side * TILE
        if self.per:
            value = take(terms, start + spot % TILE)
            keep = spot // TILE == sub
        else:
            value = take(terms, start + sub * self.sl + spot)
            keep = lane < 2 * self.sl
        return jnp.where(keep, value, 0.0)

    def spread(self, me, tile, terms, side, own_ref, sib_ref):
        if self.per:
            device = tile // self.per
            spots = [(device, tile - device * self.per)]
        else:
            spots = [(tile * self.parts + r, r) for r in range(self.parts)]
        for device, sub in spots:
            value = self.place(terms, side, sub)
            same, slot = self.owner(me, device)
            own_ref[slot] = own_ref[slot] + jnp.where(same, value, 0.0)
            sib_ref[slot] = sib_ref[slot] + jnp.where(same, 0.0, value)

    def record_of(self, raw_ref):
        pieces = [raw_ref[0, 0], raw_ref[0, 1]]
        if 2 * self.sl < LANES:
            pieces.append(jnp.zeros((self.k, LANES - 2 * self.sl), jnp.float32))
        return jnp.concatenate(pieces, axis=1)


def take(value, lanes):
    return jnp.take_along_axis(value, lanes, axis=1, mode="promise_in_bounds")


def pieces(value, count):
    result = []
    for _ in range(count):
        result.append(value.astype(jnp.bfloat16))
        value = value - result[-1].astype(jnp.float32)
    return result


def matmul(lhs, rhs):
    return jnp.dot(lhs, rhs, preferred_element_type=jnp.float32)


def eights(value):
    return [value[8 * i : 8 * i + 8] for i in range(value.shape[0] // 8)]


def pack_kernel(plan, tiles_hbm, counts_hbm, gains_hbm, targets_hbm, mult_hbm, out_ref, meta_ref, bound_ref, mrec_ref, *scratch):
    bufs, sems = scratch[:-1], scratch[-1]
    copies = [
        pltpu.make_async_copy(src, dst, sems.at[i])
        for i, (src, dst) in enumerate(zip((gains_hbm, targets_hbm, mult_hbm, tiles_hbm, counts_hbm), bufs))
    ]
    for copy in copies:
        copy.start()
    for copy in copies:
        copy.wait()
    gains_ref, targets_ref, mult_ref, tiles_ref, counts_ref = bufs
    k = plan.k
    gain = plan.record_of(gains_ref)
    target = plan.record_of(targets_ref)
    mult = plan.record_of(mult_ref)
    out_ref[:k] = gain
    out_ref[k : 2 * k] = gain - penalty * (gain - target + mult)
    mrec_ref[...] = mult
    lane = plan.lane(8)
    sub = lax.broadcasted_iota(jnp.int32, (8, LANES), 0)
    tiles = tiles_ref[...]
    counts = counts_ref[...]
    meta = jnp.zeros((8, LANES), jnp.int32)
    for base in range(0, plan.blocks, 8):
        rows = jnp.zeros((8, LANES), jnp.int32)
        for n in range(base, min(base + 8, plan.blocks)):
            one, two, count = tiles[n, 0], tiles[n, 1], counts[0, n]
            ids = jnp.where(lane // TILE % 2 == 0, one, two)
            rows = jnp.where(sub == n - base, ids, rows)
            meta = jnp.where(lane == 2 * n, one, jnp.where(lane == 2 * n + 1, two, meta))
            bound_ref[n, 0] = jnp.full((8, LANES), count, jnp.int32)
            bound_ref[n, 1] = jnp.full((8, LANES), jnp.where(one != two, plan.cells, 0), jnp.int32)
        out_ref[2 * k + base : 2 * k + base + 8] = rows.astype(jnp.float32)
    meta_ref[...] = meta


def load_kernel(plan, vis_hbm, coh_hbm, vis_ref, coh_ref, vis_buf, coh_buf, sems):
    chunks = 4
    per = plan.steps // chunks
    copies = []
    for n in range(plan.blocks):
        for c in range(chunks):
            lanes = pl.ds(c * per * LANES, per * LANES)
            copies.append(
                pltpu.make_async_copy(
                    coh_hbm.at[0, n, :, :, :, lanes],
                    coh_buf.at[n, :, :, :, lanes],
                    sems.at[n * chunks + c],
                )
            )
    last = pltpu.make_async_copy(vis_hbm.at[0], vis_buf, sems.at[plan.blocks * chunks])
    for copy in copies:
        copy.start()
    last.start()
    for n in range(plan.blocks):
        for c in range(chunks):
            copies[n * chunks + c].wait()

            def convert(t, carry, n=n, c=c):
                for index in range(c * per, (c + 1) * per):
                    lanes = pl.ds(index * LANES, LANES)
                    real = coh_buf[n, t, 0, :, lanes].astype(jnp.float32)
                    imag = coh_buf[n, t, 1, :, lanes].astype(jnp.float32)
                    q = n * plan.steps + index
                    coh_ref[q, t, 0] = real
                    coh_ref[q, t, 1] = real + imag
                    coh_ref[q, t, 2] = real - imag
                return carry

            lax.fori_loop(0, plan.times, convert, 0)
    last.wait()
    for n in range(plan.blocks):
        for part in range(2):
            value = vis_buf[n, :, part, :]
            for index in range(plan.steps):
                vis_ref[n * plan.steps + index, part] = value[:, index * LANES : (index + 1) * LANES]


def table_kernel(plan, spread_ref, narrow_ref, fold_ref):
    record = lax.broadcasted_iota(jnp.int32, (LANES, LANES), 0)
    cell = lax.broadcasted_iota(jnp.int32, (LANES, LANES), 1)
    spread = cell // TILE - record
    narrow = record // TILE - cell
    fold = TILE + record % TILE - cell
    for part in range(2):
        for index in range(plan.steps):
            span = slice((2 * index + part) * LANES, (2 * index + part + 1) * LANES)
            offset = -(part * HALF + index * GROUP)
            spread_ref[:, span] = jnp.where(spread == offset, 1.0, 0.0).astype(jnp.bfloat16)
            narrow_ref[span, :] = jnp.where(narrow == offset, 1.0, 0.0).astype(jnp.bfloat16)
        hit = jnp.where(fold == -part * HALF, 1.0, 0.0).astype(jnp.bfloat16)
        fold_ref[part * LANES : (part + 1) * LANES, :] = hit


def block_gradients(
    plan, bound_ref, tile_gains, vis_ref, coh_ref, spread_ref, narrow_ref, fold_ref,
    right_ref, wide_ref, second_ref, first_ref, model_ref, error_ref,
):
    k, times, steps = plan.k, plan.times, plan.steps
    shift = steps.bit_length() - 1
    lane_k = plan.lane()
    lane = plan.lane(8)
    sample = lax.broadcasted_iota(jnp.int32, (8, LANES), 0)
    lefts = [piece for left, _ in tile_gains for piece in pieces(left, 2)]
    lefts = matmul(jnp.concatenate(lefts, axis=0), spread_ref[...])
    for n in range(plan.blocks):
        rows = [lefts[(2 * n + i) * k : (2 * n + i + 1) * k] for i in range(2)]
        value = rows[0] + rows[1]
        for index in range(steps):
            for part in range(2):
                start = (2 * index + part) * LANES
                wide_ref[n * steps + index, part] = value[:, start : start + LANES]
    for n, (left, right) in enumerate(tile_gains):
        pairs = jnp.where(lane_k // TILE % 2 == 0, right, pltpu.roll(right, TILE, 1))
        other = pltpu.roll(pairs, HALF, 1)
        right_ref[n, 0] = jnp.where(lane_k < HALF, pairs, other)
        right_ref[n, 1] = jnp.where(lane_k < HALF, other, pairs)
        second_ref[n] = jnp.zeros((2, k, LANES), jnp.float32)

    def where_is(q):
        q = jnp.int32(q)
        return lax.shift_right_logical(q, shift), lax.bitwise_and(q, steps - 1)

    def residual(q):
        n, index = where_is(q)
        lr, li = wide_ref[q, 0], wide_ref[q, 1]
        rr, ri = right_ref[n, 0], right_ref[n, 1]
        pr = lr * rr + li * ri
        pi = li * rr - lr * ri
        ps = pr + pi
        for t in range(times):
            both = sum(eights(ps * coh_ref[q, t, 0]))
            model_ref[0, 8 * t : 8 * t + 8] = both - sum(eights(pi * coh_ref[q, t, 1]))
            model_ref[1, 8 * t : 8 * t + 8] = both - sum(eights(pr * coh_ref[q, t, 2]))
        mr, mi = (sum(model_ref[part, pl.ds(j, times, stride=8), :] for j in range(8)) for part in range(2))
        upper = index * GROUP + lane // TILE - lane % TILE
        keep = ((upper < bound_ref[n, 1]) & (sample < bound_ref[n, 0]))[:times]
        er = jnp.where(keep, vis_ref[q, 0] - mr, 0.0)
        ei = jnp.where(keep, vis_ref[q, 1] - mi, 0.0)
        slot = lax.bitwise_and(jnp.int32(q), 1)
        error_ref[slot, 0, :times] = er + ei
        error_ref[slot, 1, :times] = ei
        error_ref[slot, 2, :times] = er

    def gradient(q):
        n, index = where_is(q)
        slot = lax.bitwise_and(jnp.int32(q), 1)
        sums = [None] * 3
        for t in range(times):
            for j, c in enumerate((0, 2, 1)):
                e = error_ref[slot, j, pl.ds(t, 8, stride=0), :]
                value = [e * part for part in eights(coh_ref[q, t, c])]
                sums[j] = value if t == 0 else [x + y for x, y in zip(sums[j], value)]
        both, lone_re, lone_im = (jnp.concatenate(value, axis=0) for value in sums)
        acc_re = both - lone_re
        acc_im = both - lone_im
        lr, li = wide_ref[q, 0], wide_ref[q, 1]
        rr, ri = right_ref[n, 0], right_ref[n, 1]
        second_ref[n, 0] = second_ref[n, 0] + (acc_re * lr + acc_im * li)
        second_ref[n, 1] = second_ref[n, 1] + (acc_re * li - acc_im * lr)
        terms = jnp.concatenate([acc_re * rr - acc_im * ri, acc_re * ri + acc_im * rr], axis=1)
        lanes = pl.ds(pl.multiple_of(index * 2 * LANES, 2 * LANES), 2 * LANES)
        for i, piece in enumerate(pieces(terms, PIECES)):
            rows = pl.ds(pl.multiple_of((n * PIECES + i) * k, k), k)
            first_ref[rows, lanes] = piece

    final = plan.total - 1

    def step(q, carry):
        gradient(q)
        residual(q + 1)
        return carry

    residual(0)
    lax.fori_loop(0, final, step, 0, unroll=5)
    gradient(final)

    parts = []
    for n in range(plan.blocks):
        parts += pieces(jnp.concatenate([second_ref[n, 0], second_ref[n, 1]], axis=1), PIECES)
    value = matmul(jnp.concatenate(parts, axis=0), fold_ref[...])
    value = value + matmul(first_ref[...], narrow_ref[...])
    return [
        sum(value[(n * PIECES + i) * k : (n * PIECES + i + 1) * k] for i in range(PIECES))
        for n in range(plan.blocks)
    ]


def tile_ids(plan, meta_ref):
    meta = meta_ref[0:1, :]
    return [meta[0, i] for i in range(2 * plan.blocks)]


def first_kernel(plan, meta_ref, bound_ref, own_ref, sib_ref, vis_ref, coh_ref, spread_ref, narrow_ref, fold_ref, out_ref, *scratch):
    fixed = (vis_ref, coh_ref, spread_ref, narrow_ref, fold_ref)
    me = lax.axis_index("pair")
    records = [plan.fetch(me, own_ref, sib_ref, tile, 0) for tile in tile_ids(plan, meta_ref)]
    tile_gains = [records[2 * n : 2 * n + 2] for n in range(plan.blocks)]
    for n, terms in enumerate(block_gradients(plan, bound_ref, tile_gains, *fixed, *scratch)):
        out_ref[n] = terms


def gather_terms(plan, pay_ref, term_ref, tiles):
    k = plan.k
    labels = [tile.astype(jnp.float32) for tile in tiles]

    def add(slot, sums):
        ids_all = pay_ref[slot, 2 * k : plan.rows, :]
        for n in range(plan.blocks):
            ids = ids_all[n : n + 1]
            terms = term_ref[slot, n]
            sums = [s + jnp.where(ids == label, terms, 0.0) for s, label in zip(sums, labels)]
        return sums

    sums = [jnp.zeros((k, LANES), jnp.float32) for _ in labels]
    if plan.zn <= 4:
        for slot in range(plan.zn):
            sums = add(slot, sums)
    else:
        sums = lax.fori_loop(0, plan.zn, add, sums)
    return [s + pltpu.roll(s, LANES - TILE, 1) for s in sums]


def own_tiles(plan, me):
    if plan.per:
        return [me * plan.per + s for s in range(plan.per)]
    return [me // plan.parts]


def near_kernel(plan, step_size, meta_ref, own_ref, sib_ref, term_ref, records_ref, mine_ref):
    me = lax.axis_index("pair")
    tiles = tile_ids(plan, meta_ref)
    for i, value in enumerate(gather_terms(plan, own_ref, term_ref, tiles)):
        records_ref[i] = plan.fetch(me, own_ref, sib_ref, tiles[i], plan.k) + step_size * value
    for i, value in enumerate(gather_terms(plan, own_ref, term_ref, own_tiles(plan, me))):
        mine_ref[i] = value


def rest_kernel(plan, step_size, own_ref, sib_ref, term_ref, mine_ref, mult_ref, rest_ref):
    k = plan.k
    me = lax.axis_index("pair")
    sums = gather_terms(plan, sib_ref, term_ref, own_tiles(plan, me))
    mine = [mine_ref[i] + value for i, value in enumerate(sums)]
    if plan.per:
        own_sum = sum(plan.place(value, 0, s) for s, value in enumerate(mine))
    else:
        own_sum = plan.place(mine[0], 0, me % plan.parts)
    start = own_ref[0, :k, :]
    base = own_ref[0, k : 2 * k, :]
    pull = base - (1.0 - penalty) * start
    rest = (1.0 - penalty) * (base + step_size * own_sum) + pull
    rest_ref[0] = rest
    rest_ref[1] = rest + mult_ref[...]


def second_kernel(
    plan, step_size, meta_ref, bound_ref, sib_ref, term_ref, records_ref,
    vis_ref, coh_ref, spread_ref, narrow_ref, fold_ref, part_own_ref, part_sib_ref, *scratch,
):
    fixed = (vis_ref, coh_ref, spread_ref, narrow_ref, fold_ref)
    me = lax.axis_index("pair")
    tiles = tile_ids(plan, meta_ref)
    sums = gather_terms(plan, sib_ref, term_ref, tiles)
    records = [records_ref[i] + step_size * value for i, value in enumerate(sums)]
    tile_gains = [records[2 * n : 2 * n + 2] for n in range(plan.blocks)]
    part_own_ref[...] = jnp.zeros_like(part_own_ref)
    part_sib_ref[...] = jnp.zeros_like(part_sib_ref)
    for n, terms in enumerate(block_gradients(plan, bound_ref, tile_gains, *fixed, *scratch)):
        for side in range(2):
            plan.spread(me, tiles[2 * n + side], terms, side, part_own_ref, part_sib_ref)


def fit_kernel(plan, fit, gain_ref, own_ref, *refs):
    others, (gain_out, target_out, mult_out) = refs[:-3], refs[-3:]
    sl = plan.sl
    band = lax.axis_index("band")
    total = None
    for m, ref in enumerate((own_ref,) + tuple(others)):
        factor = jnp.float32(0.0)
        for f in range(fit.shape[0]):
            factor = jnp.where(band == f, jnp.float32(fit[f, f ^ m]), factor)
        value = factor * ref[...]
        total = value if total is None else total + value
    change = own_ref[...] - total
    gain = gain_ref[...]
    for part in range(2):
        lanes = slice(part * sl, (part + 1) * sl)
        gain_out[0, part] = gain[:, lanes]
        target_out[0, part] = total[:, lanes]
        mult_out[0, part] = change[:, lanes]


def exchange(value, axis, size, mask):
    return lax.ppermute(value, axis, [(i, i ^ mask) for i in range(size)])


def local(visibilities, coherencies, block_tiles, sample_counts, gains, targets, multipliers):
    pairs = lax.axis_size("pair")
    bands = lax.axis_size("band")
    _, blocks, times, _, directions, cells = coherencies.shape
    stations = gains.shape[3]
    plan = Plan(directions, stations, pairs, blocks, times, cells)
    k, zn = plan.k, plan.zn
    tile_count = stations * pairs // TILE
    step_size = 0.25 * tile_count * k / (times * TILE * blocks * pairs)

    vmem = pl.BlockSpec(memory_space=pltpu.VMEM)
    hbm = pl.BlockSpec(memory_space=pltpu.HBM)
    stay = lambda value: pltpu.with_memory_space_constraint(value, pltpu.HBM)
    i32 = lambda *shape: jax.ShapeDtypeStruct(shape, jnp.int32)
    f32 = lambda *shape: jax.ShapeDtypeStruct(shape, jnp.float32)
    scratch = [
        pltpu.VMEM((blocks, 2, k, LANES), jnp.float32),
        pltpu.VMEM((plan.total, 2, k, LANES), jnp.float32),
        pltpu.VMEM((blocks, 2, k, LANES), jnp.float32),
        pltpu.VMEM((blocks * PIECES * k, 2 * cells), jnp.bfloat16),
        pltpu.VMEM((2, 8 * times, LANES), jnp.float32),
        pltpu.VMEM((2, 3, 8, LANES), jnp.float32),
    ]
    params = pltpu.CompilerParams(vmem_limit_bytes=16 << 20)

    payload, meta, bounds, mult_rec = pl.pallas_call(
        lambda *refs: pack_kernel(plan, *refs),
        name="pack",
        in_specs=[hbm] * 5,
        out_specs=[vmem] * 4,
        out_shape=[f32(plan.rows, LANES), i32(8, LANES), i32(blocks, 2, 8, LANES), f32(k, LANES)],
        scratch_shapes=[pltpu.VMEM(gains.shape, jnp.float32)] * 3
        + [
            pltpu.VMEM(block_tiles.shape, jnp.int32),
            pltpu.VMEM((1, blocks), jnp.int32),
            pltpu.SemaphoreType.DMA((5,)),
        ],
        compiler_params=params,
    )(*map(stay, (block_tiles, sample_counts.reshape(1, blocks), gains, targets, multipliers)))

    vis, coh = pl.pallas_call(
        lambda *refs: load_kernel(plan, *refs),
        name="load",
        in_specs=[hbm] * 2,
        out_specs=[vmem] * 2,
        out_shape=[f32(plan.total, 2, times, LANES), f32(plan.total, times, 3, k, LANES)],
        scratch_shapes=[
            pltpu.VMEM((blocks, times, 2, cells), jnp.float32),
            pltpu.VMEM((blocks, times, 2, k, cells), jnp.bfloat16),
            pltpu.SemaphoreType.DMA((4 * blocks + 1,)),
        ],
        compiler_params=params,
    )(stay(visibilities), stay(coherencies))

    bf16 = lambda *shape: jax.ShapeDtypeStruct(shape, jnp.bfloat16)
    tables = pl.pallas_call(
        lambda *refs: table_kernel(plan, *refs),
        name="tables",
        in_specs=[],
        out_specs=[vmem] * 3,
        out_shape=[
            bf16(LANES, 2 * cells),
            bf16(2 * cells, LANES),
            bf16(2 * LANES, LANES),
        ],
        compiler_params=params,
    )()

    def gather(value):
        parts = [value] + [exchange(value, "pair", pairs, 2 * m + 1) for m in range(1, zn)]
        own = jnp.stack(parts)
        return own, exchange(own, "pair", pairs, 1)

    own, sib = gather(payload)

    terms = pl.pallas_call(
        lambda *refs: first_kernel(plan, *refs),
        name="first",
        in_specs=[vmem] * 9,
        out_specs=vmem,
        out_shape=f32(blocks, k, LANES),
        scratch_shapes=scratch,
        compiler_params=params,
    )(meta, bounds, own, sib, vis, coh, *tables)

    term_own, term_sib = gather(terms)
    records, mine = pl.pallas_call(
        lambda *refs: near_kernel(plan, step_size, *refs),
        name="near",
        in_specs=[vmem] * 4,
        out_specs=[vmem] * 2,
        out_shape=[f32(2 * blocks, k, LANES), f32(max(plan.per, 1), k, LANES)],
        compiler_params=params,
    )(meta, own, sib, term_own)
    part_own, part_sib = pl.pallas_call(
        lambda *refs: second_kernel(plan, step_size, *refs),
        name="second",
        in_specs=[vmem] * 10,
        out_specs=[vmem] * 2,
        out_shape=[f32(zn, k, LANES)] * 2,
        scratch_shapes=scratch,
        compiler_params=params,
    )(meta, bounds, sib, term_sib, records, vis, coh, *tables)

    rest = pl.pallas_call(
        lambda *refs: rest_kernel(plan, step_size, *refs),
        name="rest",
        in_specs=[vmem] * 5,
        out_specs=vmem,
        out_shape=f32(2, k, LANES),
        compiler_params=params,
    )(own, sib, term_sib, mine, mult_rec)
    crossed = exchange(part_sib, "pair", pairs, 1)
    total = part_own[0] + crossed[0]
    for m in range(1, zn):
        total = total + exchange(part_own[m] + crossed[m], "pair", pairs, 2 * m + 1)
    new_gain = rest[0] + step_size * total
    summed = rest[1] + step_size * total

    others = [exchange(summed, "band", bands, m) for m in range(1, bands)]
    shape = f32(*gains.shape)
    return pl.pallas_call(
        lambda *refs: fit_kernel(plan, fit_matrix(bands, P_SIZE), *refs),
        name="fit",
        in_specs=[vmem] * (2 + len(others)),
        out_specs=[vmem] * 3,
        out_shape=[shape] * 3,
        compiler_params=params,
    )(new_gain, summed, *others)


def solution(mesh):
    placed = (
        P("band", "pair", None, None, None),
        P("band", "pair", None, None, None, None),
        P("pair", None),
        P("pair"),
        P("band", None, None, "pair"),
        P("band", None, None, "pair"),
        P("band", None, None, "pair"),
    )
    return jax.shard_map(
        local,
        mesh=mesh,
        in_specs=placed,
        out_specs=(
            P("band", None, None, "pair"),
            P("band", None, None, "pair"),
            P("band", None, None, "pair"),
        ),
        check_vma=False,
    )
```

```python
import math

import jax
import jax.numpy as jnp
import numpy as np
from jax import lax
from jax.experimental import pallas as pl
from jax.experimental.pallas import tpu as pltpu
from jax.sharding import PartitionSpec as P


P_SIZE = 8
TILE = 32
LANES = 128
HALF = LANES // 2
GROUP = LANES // TILE
PIECES = 2

ridge = 0.05
penalty = 0.25


def fit_matrix(freq_count, term_count):
    positions = (np.arange(freq_count) + 0.5) / freq_count
    basis = np.stack(
        [
            math.comb(term_count - 1, degree)
            * positions**degree
            * (1.0 - positions) ** (term_count - 1 - degree)
            for degree in range(term_count)
        ],
        axis=1,
    )
    normal = basis.T @ basis + ridge * np.eye(term_count)
    factor = np.linalg.cholesky(normal)
    half = np.linalg.solve(factor, basis.T)
    return half.T @ half


class Plan:
    def __init__(self, directions, stations, pairs, blocks, times, cells):
        self.k = directions
        self.sl = stations
        self.zn = pairs // 2
        self.blocks = blocks
        self.times = times
        self.cells = cells
        self.steps = cells // LANES
        self.total = blocks * self.steps
        self.per = stations // TILE
        self.parts = 1 if self.per else TILE // stations
        self.rows = 2 * directions + 8 * ((blocks + 7) // 8)
        assert 2 * stations <= LANES and directions == 32 and times <= 8 and self.steps == 8

    def lane(self, rows=None):
        return lax.broadcasted_iota(jnp.int32, (self.k if rows is None else rows, LANES), 1)

    def owner(self, me, device):
        slot = lax.shift_right_logical(device ^ me, 1)
        crossed = lax.bitwise_and(device ^ me, 1)
        return crossed == jnp.where(slot == 0, 0, 1), slot

    def record(self, me, own_ref, sib_ref, device, row):
        same, slot = self.owner(me, device)
        own = own_ref[slot, row : row + self.k, :]
        sib = sib_ref[slot, row : row + self.k, :]
        return jnp.where(same, own, sib)

    def fetch(self, me, own_ref, sib_ref, tile, row):
        lane = self.lane()
        part, spot = lane // HALF, lane % TILE
        if self.sl == HALF:
            device = lax.shift_right_logical(tile, 1)
            sub = lax.bitwise_and(tile, 1)
            rec = self.record(me, own_ref, sib_ref, device, row)
            return jnp.where(sub == 1, pltpu.roll(rec, LANES - TILE, 1), rec)
        if self.per:
            device = tile // self.per
            sub = tile - device * self.per
            rec = self.record(me, own_ref, sib_ref, device, row)
            return take(rec, part * self.sl + sub * TILE + spot)
        value = None
        for r in range(self.parts):
            rec = self.record(me, own_ref, sib_ref, tile * self.parts + r, row)
            here = take(rec, part * self.sl + spot % self.sl)
            value = here if value is None else jnp.where(spot // self.sl == r, here, value)
        return value

    def place(self, terms, side, sub):
        lane = self.lane()
        if self.sl == HALF:
            moved = pltpu.roll(terms, TILE if side == 0 else LANES - TILE, 1)
            return jnp.where(lane // TILE % 2 == sub, jnp.where(sub == side, terms, moved), 0.0)
        part, spot = lane // self.sl % 2, lane % self.sl
        start = part * HALF + side * TILE
        if self.per:
            value = take(terms, start + spot % TILE)
            keep = spot // TILE == sub
        else:
            value = take(terms, start + sub * self.sl + spot)
            keep = lane < 2 * self.sl
        return jnp.where(keep, value, 0.0)

    def spread(self, me, tile, terms, side, own_ref, sib_ref):
        if self.per:
            device = tile // self.per
            spots = [(device, tile - device * self.per)]
        else:
            spots = [(tile * self.parts + r, r) for r in range(self.parts)]
        for device, sub in spots:
            value = self.place(terms, side, sub)
            same, slot = self.owner(me, device)
            own_ref[slot] = own_ref[slot] + jnp.where(same, value, 0.0)
            sib_ref[slot] = sib_ref[slot] + jnp.where(same, 0.0, value)

    def record_of(self, raw_ref):
        pieces = [raw_ref[0, 0], raw_ref[0, 1]]
        if 2 * self.sl < LANES:
            pieces.append(jnp.zeros((self.k, LANES - 2 * self.sl), jnp.float32))
        return jnp.concatenate(pieces, axis=1)


def take(value, lanes):
    return jnp.take_along_axis(value, lanes, axis=1, mode="promise_in_bounds")


def pieces(value, count):
    result = []
    for _ in range(count):
        result.append(value.astype(jnp.bfloat16))
        value = value - result[-1].astype(jnp.float32)
    return result


def matmul(lhs, rhs):
    return jnp.dot(lhs, rhs, preferred_element_type=jnp.float32)


def eights(value):
    return [value[8 * i : 8 * i + 8] for i in range(value.shape[0] // 8)]


def pack_kernel(plan, tiles_hbm, counts_hbm, gains_hbm, targets_hbm, mult_hbm, out_ref, meta_ref, bound_ref, mrec_ref, *scratch):
    bufs, sems = scratch[:-1], scratch[-1]
    copies = [
        pltpu.make_async_copy(src, dst, sems.at[i])
        for i, (src, dst) in enumerate(zip((gains_hbm, targets_hbm, mult_hbm, tiles_hbm, counts_hbm), bufs))
    ]
    for copy in copies:
        copy.start()
    for copy in copies:
        copy.wait()
    gains_ref, targets_ref, mult_ref, tiles_ref, counts_ref = bufs
    k = plan.k
    gain = plan.record_of(gains_ref)
    target = plan.record_of(targets_ref)
    mult = plan.record_of(mult_ref)
    out_ref[:k] = gain
    out_ref[k : 2 * k] = gain - penalty * (gain - target + mult)
    mrec_ref[...] = mult
    lane = plan.lane(8)
    sub = lax.broadcasted_iota(jnp.int32, (8, LANES), 0)
    tiles = tiles_ref[...]
    counts = counts_ref[...]
    meta = jnp.zeros((8, LANES), jnp.int32)
    for base in range(0, plan.blocks, 8):
        rows = jnp.zeros((8, LANES), jnp.int32)
        for n in range(base, min(base + 8, plan.blocks)):
            one, two, count = tiles[n, 0], tiles[n, 1], counts[0, n]
            ids = jnp.where(lane // TILE % 2 == 0, one, two)
            rows = jnp.where(sub == n - base, ids, rows)
            meta = jnp.where(lane == 2 * n, one, jnp.where(lane == 2 * n + 1, two, meta))
            bound_ref[n, 0] = jnp.full((8, LANES), count, jnp.int32)
            bound_ref[n, 1] = jnp.full((8, LANES), jnp.where(one != two, plan.cells, 0), jnp.int32)
        out_ref[2 * k + base : 2 * k + base + 8] = rows.astype(jnp.float32)
    meta_ref[...] = meta


def load_kernel(plan, vis_hbm, coh_hbm, vis_ref, coh_ref, vis_buf, coh_buf, sems):
    chunks = 8
    per = plan.steps // chunks
    copies = []
    for n in range(plan.blocks):
        for c in range(chunks):
            lanes = pl.ds(c * per * LANES, per * LANES)
            copies.append(
                pltpu.make_async_copy(
                    coh_hbm.at[0, n, :, :, :, lanes],
                    coh_buf.at[n, :, :, :, lanes],
                    sems.at[n * chunks + c],
                )
            )
    last = pltpu.make_async_copy(vis_hbm.at[0], vis_buf, sems.at[plan.blocks * chunks])
    for copy in copies:
        copy.start()
    last.start()
    for n in range(plan.blocks):
        for c in range(chunks):
            copies[n * chunks + c].wait()

            def convert(t, carry, n=n, c=c):
                for index in range(c * per, (c + 1) * per):
                    lanes = pl.ds(index * LANES, LANES)
                    real = coh_buf[n, t, 0, :, lanes].astype(jnp.float32)
                    imag = coh_buf[n, t, 1, :, lanes].astype(jnp.float32)
                    q = n * plan.steps + index
                    coh_ref[q, t, 0] = real
                    coh_ref[q, t, 1] = real + imag
                    coh_ref[q, t, 2] = real - imag
                return carry

            lax.fori_loop(0, plan.times, convert, 0)
    last.wait()
    for n in range(plan.blocks):
        for part in range(2):
            value = vis_buf[n, :, part, :]
            for index in range(plan.steps):
                vis_ref[n * plan.steps + index, part] = value[:, index * LANES : (index + 1) * LANES]


def table_kernel(plan, spread_ref, narrow_ref, fold_ref):
    record = lax.broadcasted_iota(jnp.int32, (LANES, LANES), 0)
    cell = lax.broadcasted_iota(jnp.int32, (LANES, LANES), 1)
    spread = cell // TILE - record
    narrow = record // TILE - cell
    fold = TILE + record % TILE - cell
    for part in range(2):
        for index in range(plan.steps):
            span = slice((2 * index + part) * LANES, (2 * index + part + 1) * LANES)
            offset = -(part * HALF + index * GROUP)
            spread_ref[:, span] = jnp.where(spread == offset, 1.0, 0.0).astype(jnp.bfloat16)
            narrow_ref[span, :] = jnp.where(narrow == offset, 1.0, 0.0).astype(jnp.bfloat16)
        hit = jnp.where(fold == -part * HALF, 1.0, 0.0).astype(jnp.bfloat16)
        fold_ref[part * LANES : (part + 1) * LANES, :] = hit


def block_gradients(
    plan, bound_ref, tile_gains, vis_ref, coh_ref, spread_ref, narrow_ref, fold_ref,
    right_ref, wide_ref, second_ref, first_ref, model_ref, error_ref,
):
    k, times, steps = plan.k, plan.times, plan.steps
    shift = steps.bit_length() - 1
    lane_k = plan.lane()
    lane = plan.lane(8)
    sample = lax.broadcasted_iota(jnp.int32, (8, LANES), 0)
    lefts = [piece for left, _ in tile_gains for piece in pieces(left, 2)]
    lefts = matmul(jnp.concatenate(lefts, axis=0), spread_ref[...])
    for n in range(plan.blocks):
        rows = [lefts[(2 * n + i) * k : (2 * n + i + 1) * k] for i in range(2)]
        value = rows[0] + rows[1]
        for index in range(steps):
            for part in range(2):
                start = (2 * index + part) * LANES
                wide_ref[n * steps + index, part] = value[:, start : start + LANES]
    for n, (left, right) in enumerate(tile_gains):
        pairs = jnp.where(lane_k // TILE % 2 == 0, right, pltpu.roll(right, TILE, 1))
        other = pltpu.roll(pairs, HALF, 1)
        right_ref[n, 0] = jnp.where(lane_k < HALF, pairs, other)
        right_ref[n, 1] = jnp.where(lane_k < HALF, other, pairs)
        second_ref[n] = jnp.zeros((2, k, LANES), jnp.float32)

    def where_is(q):
        q = jnp.int32(q)
        return lax.shift_right_logical(q, shift), lax.bitwise_and(q, steps - 1)

    def residual(q):
        n, index = where_is(q)
        lr, li = wide_ref[q, 0], wide_ref[q, 1]
        rr, ri = right_ref[n, 0], right_ref[n, 1]
        pr = lr * rr + li * ri
        pi = li * rr - lr * ri
        ps = pr + pi
        for t in range(times):
            both = sum(eights(ps * coh_ref[q, t, 0]))
            model_ref[0, 8 * t : 8 * t + 8] = both - sum(eights(pi * coh_ref[q, t, 1]))
            model_ref[1, 8 * t : 8 * t + 8] = both - sum(eights(pr * coh_ref[q, t, 2]))
        mr, mi = (sum(model_ref[part, pl.ds(j, times, stride=8), :] for j in range(8)) for part in range(2))
        upper = index * GROUP + lane // TILE - lane % TILE
        keep = ((upper < bound_ref[n, 1]) & (sample < bound_ref[n, 0]))[:times]
        er = jnp.where(keep, vis_ref[q, 0] - mr, 0.0)
        ei = jnp.where(keep, vis_ref[q, 1] - mi, 0.0)
        slot = lax.bitwise_and(jnp.int32(q), 1)
        error_ref[slot, 0, :times] = er + ei
        error_ref[slot, 1, :times] = ei
        error_ref[slot, 2, :times] = er

    def gradient(q):
        n, index = where_is(q)
        slot = lax.bitwise_and(jnp.int32(q), 1)
        sums = [None] * 3
        for t in range(times):
            for j, c in enumerate((0, 2, 1)):
                e = error_ref[slot, j, pl.ds(t, 8, stride=0), :]
                value = [e * part for part in eights(coh_ref[q, t, c])]
                sums[j] = value if t == 0 else [x + y for x, y in zip(sums[j], value)]
        both, lone_re, lone_im = (jnp.concatenate(value, axis=0) for value in sums)
        acc_re = both - lone_re
        acc_im = both - lone_im
        lr, li = wide_ref[q, 0], wide_ref[q, 1]
        rr, ri = right_ref[n, 0], right_ref[n, 1]
        second_ref[n, 0] = second_ref[n, 0] + (acc_re * lr + acc_im * li)
        second_ref[n, 1] = second_ref[n, 1] + (acc_re * li - acc_im * lr)
        terms = jnp.concatenate([acc_re * rr - acc_im * ri, acc_re * ri + acc_im * rr], axis=1)
        lanes = pl.ds(pl.multiple_of(index * 2 * LANES, 2 * LANES), 2 * LANES)
        for i, piece in enumerate(pieces(terms, PIECES)):
            rows = pl.ds(pl.multiple_of((n * PIECES + i) * k, k), k)
            first_ref[rows, lanes] = piece

    final = plan.total - 1

    def step(q, carry):
        gradient(q)
        residual(q + 1)
        return carry

    residual(0)
    lax.fori_loop(0, final, step, 0, unroll=5)
    gradient(final)

    parts = []
    for n in range(plan.blocks):
        parts += pieces(jnp.concatenate([second_ref[n, 0], second_ref[n, 1]], axis=1), PIECES)
    value = matmul(jnp.concatenate(parts, axis=0), fold_ref[...])
    value = value + matmul(first_ref[...], narrow_ref[...])
    return [
        sum(value[(n * PIECES + i) * k : (n * PIECES + i + 1) * k] for i in range(PIECES))
        for n in range(plan.blocks)
    ]


def tile_ids(plan, meta_ref):
    meta = meta_ref[0:1, :]
    return [meta[0, i] for i in range(2 * plan.blocks)]


def first_kernel(plan, meta_ref, bound_ref, own_ref, sib_ref, vis_ref, coh_ref, spread_ref, narrow_ref, fold_ref, out_ref, *scratch):
    fixed = (vis_ref, coh_ref, spread_ref, narrow_ref, fold_ref)
    me = lax.axis_index("pair")
    records = [plan.fetch(me, own_ref, sib_ref, tile, 0) for tile in tile_ids(plan, meta_ref)]
    tile_gains = [records[2 * n : 2 * n + 2] for n in range(plan.blocks)]
    for n, terms in enumerate(block_gradients(plan, bound_ref, tile_gains, *fixed, *scratch)):
        out_ref[n] = terms


def gather_terms(plan, pay_ref, term_ref, tiles):
    k = plan.k
    labels = [tile.astype(jnp.float32) for tile in tiles]

    def add(slot, sums):
        ids_all = pay_ref[slot, 2 * k : plan.rows, :]
        for n in range(plan.blocks):
            ids = ids_all[n : n + 1]
            terms = term_ref[slot, n]
            sums = [s + jnp.where(ids == label, terms, 0.0) for s, label in zip(sums, labels)]
        return sums

    sums = [jnp.zeros((k, LANES), jnp.float32) for _ in labels]
    if plan.zn <= 4:
        for slot in range(plan.zn):
            sums = add(slot, sums)
    else:
        sums = lax.fori_loop(0, plan.zn, add, sums)
    return [s + pltpu.roll(s, LANES - TILE, 1) for s in sums]


def own_tiles(plan, me):
    if plan.per:
        return [me * plan.per + s for s in range(plan.per)]
    return [me // plan.parts]


def near_kernel(plan, step_size, meta_ref, own_ref, sib_ref, term_ref, records_ref, mine_ref):
    me = lax.axis_index("pair")
    tiles = tile_ids(plan, meta_ref)
    for i, value in enumerate(gather_terms(plan, own_ref, term_ref, tiles)):
        records_ref[i] = plan.fetch(me, own_ref, sib_ref, tiles[i], plan.k) + step_size * value
    for i, value in enumerate(gather_terms(plan, own_ref, term_ref, own_tiles(plan, me))):
        mine_ref[i] = value


def rest_kernel(plan, step_size, own_ref, sib_ref, term_ref, mine_ref, mult_ref, rest_ref):
    k = plan.k
    me = lax.axis_index("pair")
    sums = gather_terms(plan, sib_ref, term_ref, own_tiles(plan, me))
    mine = [mine_ref[i] + value for i, value in enumerate(sums)]
    if plan.per:
        own_sum = sum(plan.place(value, 0, s) for s, value in enumerate(mine))
    else:
        own_sum = plan.place(mine[0], 0, me % plan.parts)
    start = own_ref[0, :k, :]
    base = own_ref[0, k : 2 * k, :]
    pull = base - (1.0 - penalty) * start
    rest = (1.0 - penalty) * (base + step_size * own_sum) + pull
    rest_ref[0] = rest
    rest_ref[1] = rest + mult_ref[...]


def second_kernel(
    plan, step_size, meta_ref, bound_ref, sib_ref, term_ref, records_ref,
    vis_ref, coh_ref, spread_ref, narrow_ref, fold_ref, part_own_ref, part_sib_ref, *scratch,
):
    fixed = (vis_ref, coh_ref, spread_ref, narrow_ref, fold_ref)
    me = lax.axis_index("pair")
    tiles = tile_ids(plan, meta_ref)
    sums = gather_terms(plan, sib_ref, term_ref, tiles)
    records = [records_ref[i] + step_size * value for i, value in enumerate(sums)]
    tile_gains = [records[2 * n : 2 * n + 2] for n in range(plan.blocks)]
    part_own_ref[...] = jnp.zeros_like(part_own_ref)
    part_sib_ref[...] = jnp.zeros_like(part_sib_ref)
    for n, terms in enumerate(block_gradients(plan, bound_ref, tile_gains, *fixed, *scratch)):
        for side in range(2):
            plan.spread(me, tiles[2 * n + side], terms, side, part_own_ref, part_sib_ref)


def emit_kernel(plan, gain_ref, gain_out):
    gain = gain_ref[...]
    for part in range(2):
        gain_out[0, part] = gain[:, part * plan.sl : (part + 1) * plan.sl]


def fit_kernel(plan, fit, own_ref, *refs):
    others, (target_out, mult_out) = refs[:-2], refs[-2:]
    sl = plan.sl
    band = lax.axis_index("band")
    total = None
    for m, ref in enumerate((own_ref,) + tuple(others)):
        factor = jnp.float32(0.0)
        for f in range(fit.shape[0]):
            factor = jnp.where(band == f, jnp.float32(fit[f, f ^ m]), factor)
        value = factor * ref[...]
        total = value if total is None else total + value
    change = own_ref[...] - total
    for part in range(2):
        lanes = slice(part * sl, (part + 1) * sl)
        target_out[0, part] = total[:, lanes]
        mult_out[0, part] = change[:, lanes]


def exchange(value, axis, size, mask):
    return lax.ppermute(value, axis, [(i, i ^ mask) for i in range(size)])


def local(visibilities, coherencies, block_tiles, sample_counts, gains, targets, multipliers):
    pairs = lax.axis_size("pair")
    bands = lax.axis_size("band")
    _, blocks, times, _, directions, cells = coherencies.shape
    stations = gains.shape[3]
    plan = Plan(directions, stations, pairs, blocks, times, cells)
    k, zn = plan.k, plan.zn
    tile_count = stations * pairs // TILE
    step_size = 0.25 * tile_count * k / (times * TILE * blocks * pairs)

    vmem = pl.BlockSpec(memory_space=pltpu.VMEM)
    hbm = pl.BlockSpec(memory_space=pltpu.HBM)
    stay = lambda value: pltpu.with_memory_space_constraint(value, pltpu.HBM)
    i32 = lambda *shape: jax.ShapeDtypeStruct(shape, jnp.int32)
    f32 = lambda *shape: jax.ShapeDtypeStruct(shape, jnp.float32)
    scratch = [
        pltpu.VMEM((blocks, 2, k, LANES), jnp.float32),
        pltpu.VMEM((plan.total, 2, k, LANES), jnp.float32),
        pltpu.VMEM((blocks, 2, k, LANES), jnp.float32),
        pltpu.VMEM((blocks * PIECES * k, 2 * cells), jnp.bfloat16),
        pltpu.VMEM((2, 8 * times, LANES), jnp.float32),
        pltpu.VMEM((2, 3, 8, LANES), jnp.float32),
    ]
    params = pltpu.CompilerParams(vmem_limit_bytes=16 << 20)

    payload, meta, bounds, mult_rec = pl.pallas_call(
        lambda *refs: pack_kernel(plan, *refs),
        name="pack",
        in_specs=[hbm] * 5,
        out_specs=[vmem] * 4,
        out_shape=[f32(plan.rows, LANES), i32(8, LANES), i32(blocks, 2, 8, LANES), f32(k, LANES)],
        scratch_shapes=[pltpu.VMEM(gains.shape, jnp.float32)] * 3
        + [
            pltpu.VMEM(block_tiles.shape, jnp.int32),
            pltpu.VMEM((1, blocks), jnp.int32),
            pltpu.SemaphoreType.DMA((5,)),
        ],
        compiler_params=params,
    )(*map(stay, (block_tiles, sample_counts.reshape(1, blocks), gains, targets, multipliers)))

    vis, coh = pl.pallas_call(
        lambda *refs: load_kernel(plan, *refs),
        name="load",
        in_specs=[hbm] * 2,
        out_specs=[vmem] * 2,
        out_shape=[f32(plan.total, 2, times, LANES), f32(plan.total, times, 3, k, LANES)],
        scratch_shapes=[
            pltpu.VMEM((blocks, times, 2, cells), jnp.float32),
            pltpu.VMEM((blocks, times, 2, k, cells), jnp.bfloat16),
            pltpu.SemaphoreType.DMA((8 * blocks + 1,)),
        ],
        compiler_params=params,
    )(stay(visibilities), stay(coherencies))

    bf16 = lambda *shape: jax.ShapeDtypeStruct(shape, jnp.bfloat16)
    tables = pl.pallas_call(
        lambda *refs: table_kernel(plan, *refs),
        name="tables",
        in_specs=[],
        out_specs=[vmem] * 3,
        out_shape=[
            bf16(LANES, 2 * cells),
            bf16(2 * cells, LANES),
            bf16(2 * LANES, LANES),
        ],
        compiler_params=params,
    )()

    def gather(value):
        parts = [value] + [exchange(value, "pair", pairs, 2 * m + 1) for m in range(1, zn)]
        own = jnp.stack(parts)
        return own, exchange(own, "pair", pairs, 1)

    own, sib = gather(payload)

    terms = pl.pallas_call(
        lambda *refs: first_kernel(plan, *refs),
        name="first",
        in_specs=[vmem] * 9,
        out_specs=vmem,
        out_shape=f32(blocks, k, LANES),
        scratch_shapes=scratch,
        compiler_params=params,
    )(meta, bounds, own, sib, vis, coh, *tables)

    term_own, term_sib = gather(terms)
    records, mine = pl.pallas_call(
        lambda *refs: near_kernel(plan, step_size, *refs),
        name="near",
        in_specs=[vmem] * 4,
        out_specs=[vmem] * 2,
        out_shape=[f32(2 * blocks, k, LANES), f32(max(plan.per, 1), k, LANES)],
        compiler_params=params,
    )(meta, own, sib, term_own)
    part_own, part_sib = pl.pallas_call(
        lambda *refs: second_kernel(plan, step_size, *refs),
        name="second",
        in_specs=[vmem] * 10,
        out_specs=[vmem] * 2,
        out_shape=[f32(zn, k, LANES)] * 2,
        scratch_shapes=scratch,
        compiler_params=params,
    )(meta, bounds, sib, term_sib, records, vis, coh, *tables)

    rest = pl.pallas_call(
        lambda *refs: rest_kernel(plan, step_size, *refs),
        name="rest",
        in_specs=[vmem] * 5,
        out_specs=vmem,
        out_shape=f32(2, k, LANES),
        compiler_params=params,
    )(own, sib, term_sib, mine, mult_rec)
    crossed = exchange(part_sib, "pair", pairs, 1)
    total = part_own[0] + crossed[0]
    for m in range(1, zn):
        total = total + exchange(part_own[m] + crossed[m], "pair", pairs, 2 * m + 1)
    new_gain = rest[0] + step_size * total
    summed = rest[1] + step_size * total

    others = [exchange(summed, "band", bands, m) for m in range(1, bands)]
    emitted = pl.pallas_call(
        lambda *refs: emit_kernel(plan, *refs),
        name="emit",
        in_specs=[vmem],
        out_specs=vmem,
        out_shape=f32(*gains.shape),
        compiler_params=params,
    )(new_gain)
    shape = f32(*gains.shape)
    fitted, change = pl.pallas_call(
        lambda *refs: fit_kernel(plan, fit_matrix(bands, P_SIZE), *refs),
        name="fit",
        in_specs=[vmem] * (1 + len(others)),
        out_specs=[vmem] * 2,
        out_shape=[shape] * 2,
        compiler_params=params,
    )(summed, *others)
    return emitted, fitted, change


def solution(mesh):
    placed = (
        P("band", "pair", None, None, None),
        P("band", "pair", None, None, None, None),
        P("pair", None),
        P("pair"),
        P("band", None, None, "pair"),
        P("band", None, None, "pair"),
        P("band", None, None, "pair"),
    )
    return jax.shard_map(
        local,
        mesh=mesh,
        in_specs=placed,
        out_specs=(
            P("band", None, None, "pair"),
            P("band", None, None, "pair"),
            P("band", None, None, "pair"),
        ),
        check_vma=False,
    )
```
